128 devices in a mesh: visit: 4 (over y), patch: 32 (over x, z, core).
Axes of the slice: x: 4, y: 4, z: 4, core: 2. Of those that a mesh axis runs over, the one named last changes fastest.
Arguments:
- image: float32 [4, 32, 32, 128, 128], P('visit', 'patch'), may hold values from -6 to 6
- variance: float32 [4, 32, 32, 128, 128], P('visit', 'patch'), may hold values from 4 to 64
- dest_patch: int32 [4, 32, 32], P('visit', 'patch'), may hold values from 0 to 31, as said below
- quadrant: int32 [4, 32, 32], P('visit', 'patch'), may hold values from 0 to 3
- coef_index: int32 [4, 32, 32], P('visit', 'patch'), may hold values from 0 to 799
- block_count: int32 [4, 32], P('visit', 'patch'), may hold values from 24 to 32, as said below
- coef_table: float32 [800, 16, 6], replicated, may hold values from -0.625 to 0.625
- row_taps: float32 [16, 41], replicated, may hold values from -1 to 1
- col_taps: float32 [16, 41], replicated, may hold values from -1 to 1
Outputs:
- weighted_sum: float32 [32, 256, 256], P('patch', 'visit')
- weight_sum: float32 [32, 256, 256], P('patch', 'visit')
The draws below stay inside these ranges and needn't reach their ends.
Inputs may be any that keep to these rules, and one draw needn't show every extreme that they name: `dest_patch`: among the blocks of one device at most 2 name the same patch slice; one patch slice, drawn from the seed, is named by exactly 2 live blocks of every device. `block_count`: some device has all 32 blocks live.
All inputs are finite; a program needn't handle non-finite values.
Results may differ from the reference program's by a relative error of at most 0.0003.
Values sent between devices are 32-bit elements; how exact they have to be, the bound alone decides.
A program may use at most 192 MiB of HBM per device.

```python
import math
import jax
import jax.numpy as jnp
from jax import lax

BLOCK = 128
BLK_DEV = 32
TAPS = 41
NBASIS = 16
NPOLY = 6
NTAB = 800
CAP = 2
N_VISIT = 4
N_PATCH = 32


def draw_dest_patch(key, part):
    slot_total = N_PATCH * CAP
    key_heavy, key_favour, key_score, key_order = jax.random.split(key, 4)
    heavy_owner = jax.random.randint(key_heavy, (), 0, N_PATCH)
    favour = jax.random.randint(key_favour, (N_PATCH,), 1, 5)
    slot_owner = jnp.arange(slot_total) // CAP
    random_part = jax.random.randint(key_score, (N_VISIT, N_PATCH, slot_total), 0, 1000)
    slot_score = random_part * favour[slot_owner][None, None, :] + 5000 * (slot_owner == heavy_owner).astype(jnp.int32)[None, None, :]
    slot_score = slot_score * slot_total + jnp.arange(slot_total)[None, None, :]
    best_score, chosen = lax.top_k(slot_score, BLK_DEV)
    targets = chosen // CAP
    live_front = 3 * BLK_DEV // 4
    position = jnp.arange(BLK_DEV)
    shuffle = jax.random.randint(key_order, (N_VISIT, N_PATCH, BLK_DEV), 0, 1 << 20)
    sort_key = jnp.where(position[None, None, :] < live_front, shuffle * BLK_DEV + position[None, None, :], (1 << 20) * BLK_DEV + position[None, None, :])
    placing = jnp.argsort(sort_key, axis=-1, stable=True)
    return jnp.take_along_axis(targets, placing, axis=-1).astype(jnp.int32)


def draw_block_count(key, part):
    key_counts, key_full = jax.random.split(key)
    live_counts = jax.random.randint(key_counts, (N_VISIT, N_PATCH), 3 * BLK_DEV // 4, BLK_DEV + 1)
    full_cell = jax.random.randint(key_full, (), 0, N_VISIT * N_PATCH)
    flat_counts = jnp.where(jnp.arange(N_VISIT * N_PATCH) == full_cell, BLK_DEV, live_counts.reshape(-1))
    return flat_counts.reshape(N_VISIT, N_PATCH).astype(jnp.int32)


def place_ends(values, own_key, least, high):
    extent = values.shape
    index_at = [jax.random.randint(jax.random.fold_in(own_key, axis), (), 0, extent[axis]) for axis in range(len(extent))]
    values = values.at[tuple(index_at)].set(least)
    longest = extent.index(max(extent))
    index_at[longest] = (index_at[longest] + 1) % extent[longest]
    return values.at[tuple(index_at)].set(high)


def steps_of(own_key, shape, pieces, low, top_value):
    def one(dim, shards_of):
        heights = jax.random.uniform(jax.random.fold_in(jax.random.fold_in(own_key, 6), dim), (shards_of,), jnp.float32, low / len(pieces), top_value / len(pieces))
        return jnp.repeat(jnp.exp(heights), shape[dim] // shards_of).reshape((-1,) + (1,) * (len(shape) - dim - 1))

    factor_of = one(*pieces[0])
    for cut in pieces[1:]:
        factor_of = factor_of * one(*cut)
    return factor_of


def bell_draw(key, shape, deviation, reach, cuts=(), dtype=jnp.bfloat16):
    loudness = steps_of(key, shape, cuts, -0.22, 0.18) if cuts else 1.0
    result = jax.random.normal(key, shape, jnp.float32) * deviation * loudness
    return jnp.minimum(jnp.maximum(result, -reach), reach).astype(dtype)


def setup_inputs(seed: int = 0) -> dict:
    key_of = jax.random.split(jax.random.key(seed), 10)
    image = bell_draw(key_of[0], (N_VISIT, N_PATCH, BLK_DEV, BLOCK, BLOCK), 1.0, 6.0, ((0, 4), (1, 32)), jnp.float32)
    variance = jnp.clip(jnp.exp(math.log(64.0) - 2.7725887 * jax.random.uniform(key_of[1], (N_VISIT, N_PATCH, BLK_DEV, BLOCK, BLOCK), jnp.float32) ** steps_of(key_of[1], (N_VISIT, N_PATCH, BLK_DEV, BLOCK, BLOCK), ((0, 4), (1, 32)), -0.2, 0.2)), 4.0, 64.0)
    dest_patch = draw_dest_patch(jax.random.fold_in(key_of[9], 71), 0)
    quadrant = place_ends(jax.random.randint(key_of[3], (N_VISIT, N_PATCH, BLK_DEV), 0, 4), jax.random.fold_in(key_of[3], 1), 0, 3).astype(jnp.int32)
    coef_index = place_ends(jax.random.randint(key_of[4], (N_VISIT, N_PATCH, BLK_DEV), 0, NTAB), jax.random.fold_in(key_of[4], 1), 0, NTAB - 1).astype(jnp.int32)
    block_count = draw_block_count(jax.random.fold_in(key_of[9], 71), 0)
    coef_table = bell_draw(key_of[6], (NTAB, NBASIS, NPOLY), (NBASIS * NPOLY) ** -0.5, 0.625, (), jnp.float32)
    row_taps = bell_draw(key_of[7], (NBASIS, TAPS), TAPS ** -0.5, 1.0, (), jnp.float32)
    col_taps = bell_draw(key_of[8], (NBASIS, TAPS), TAPS ** -0.5, 1.0, (), jnp.float32)
    return {"image": image, "variance": variance, "dest_patch": dest_patch, "quadrant": quadrant, "coef_index": coef_index, "block_count": block_count, "coef_table": coef_table, "row_taps": row_taps, "col_taps": col_taps}


highest = lax.Precision.HIGHEST


def band_matrices(filter_taps, block_side, reversed_band):
    radius = (filter_taps.shape[1] - 1) // 2
    row_index = jnp.arange(block_side)[:, None]
    col_index = jnp.arange(block_side)[None, :]
    offset = row_index - col_index if reversed_band else col_index - row_index
    banded = jnp.zeros((filter_taps.shape[0], block_side, block_side), jnp.float32)
    for tap_index in range(filter_taps.shape[1]):
        picked = (offset == tap_index - radius).astype(jnp.float32)
        banded = banded + filter_taps[:, tap_index, None, None] * picked[None, :, :]
    return banded


def match_blocks(pixels, coefficients, down_quarter, across_quarter, row_band, col_band):
    block_side = pixels.shape[-1]
    pixel_index = jnp.arange(block_side).astype(jnp.float32)
    across_pos = ((across_quarter[:, None] * block_side + pixel_index[None, :]) + 0.5) / block_side - 1.0
    down_pos = ((down_quarter[:, None] * block_side + pixel_index[None, :]) + 0.5) / block_side - 1.0
    across_pos = across_pos[:, None, :]
    down_pos = down_pos[:, :, None]
    matched = jnp.zeros(pixels.shape, jnp.float32)
    for basis_index in range(row_band.shape[0]):
        spread = jnp.einsum("nij,jk->nik", pixels, row_band[basis_index], precision=highest, preferred_element_type=jnp.float32)
        convolved = jnp.einsum("ij,njk->nik", col_band[basis_index], spread, precision=highest, preferred_element_type=jnp.float32)
        poly_terms = coefficients[:, basis_index, :]
        weight = (poly_terms[:, 0, None, None] + poly_terms[:, 1, None, None] * across_pos
                  + poly_terms[:, 2, None, None] * down_pos + poly_terms[:, 3, None, None] * across_pos * across_pos
                  + poly_terms[:, 4, None, None] * across_pos * down_pos + poly_terms[:, 5, None, None] * down_pos * down_pos)
        matched = matched + weight * convolved
    return matched


def reference(image, variance, dest_patch, quadrant, coef_index, block_count, coef_table, row_taps, col_taps):
    block_side = image.shape[-1]
    row_band = band_matrices(row_taps, block_side, False)
    col_band = band_matrices(col_taps, block_side, True)
    devices_all = image.shape[0] * image.shape[1]
    blocks = image.shape[2]
    live_mask = jnp.arange(blocks)[None, None, :] < block_count[:, :, None]
    stacked = (image.reshape(devices_all, blocks, block_side, block_side),
               variance.reshape(devices_all, blocks, block_side, block_side),
               dest_patch.reshape(devices_all, blocks).astype(jnp.int32),
               quadrant.reshape(devices_all, blocks).astype(jnp.int32),
               coef_index.reshape(devices_all, blocks).astype(jnp.int32),
               live_mask.reshape(devices_all, blocks))
    start = (jnp.zeros((N_PATCH, 2, block_side, 2, block_side), jnp.float32),
             jnp.zeros((N_PATCH, 2, block_side, 2, block_side), jnp.float32))

    def add_device(running, device_item):
        weighted, weight_total = running
        pixels, variances, targets, quadrants, table_rows, is_live = device_item
        down_quarter = (quadrants // 2).astype(jnp.float32)
        across_quarter = (quadrants % 2).astype(jnp.float32)
        matched = match_blocks(pixels, coef_table[table_rows], down_quarter, across_quarter, row_band, col_band)
        inverse = is_live.astype(jnp.float32)[:, None, None] / variances
        weighted = weighted.at[targets, quadrants // 2, :, quadrants % 2, :].add(inverse * matched)
        weight_total = weight_total.at[targets, quadrants // 2, :, quadrants % 2, :].add(inverse)
        return (weighted, weight_total), None

    (weighted, weight_total), unused = lax.scan(add_device, start, stacked)
    return (weighted.reshape(N_PATCH, 2 * block_side, 2 * block_side),
            weight_total.reshape(N_PATCH, 2 * block_side, 2 * block_side))
```

```python
import functools

import jax
import jax.numpy as jnp
from jax import lax
from jax.experimental import pallas as pl
from jax.experimental.pallas import tpu as pltpu
from jax.sharding import PartitionSpec as P

highest = lax.Precision.HIGHEST
BLOCK = 128
TAPS = 41
NB = 16
TILE = 32
WIN = 80
LEAD = 24
GROUP = 8


def split(x):
    high = x.astype(jnp.bfloat16)
    return high, (x - high.astype(jnp.float32)).astype(jnp.bfloat16)


def split_outside(x):
    high = lax.reduce_precision(x, exponent_bits=8, mantissa_bits=7)
    return high.astype(jnp.bfloat16), (x - high).astype(jnp.bfloat16)


def toeplitz(taps, rows, columns, tap_of):
    at = tap_of(jnp.arange(rows)[:, None], jnp.arange(columns)[None, :])
    banded = jnp.zeros((taps.shape[0], rows, columns), jnp.float32)
    for tap in range(TAPS):
        banded = banded + taps[:, tap, None, None] * (at == tap).astype(jnp.float32)[None]
    return banded


def bands(row_taps, col_taps):
    col = toeplitz(col_taps, TILE, WIN, lambda r, s: r - s + LEAD + TAPS // 2)
    high, low = split_outside(col)
    left = jnp.concatenate([high, low, high, jnp.zeros((NB, TILE, 256 - 3 * WIN), jnp.bfloat16)], axis=2)
    left = left.reshape(NB * TILE, 256)
    row = toeplitz(row_taps, BLOCK, BLOCK, lambda i, j: j - i + TAPS // 2)
    high, low = split_outside(row)
    top = jnp.concatenate([high, low], axis=2)
    bottom = jnp.concatenate([high, jnp.zeros_like(low)], axis=2)
    return left, jnp.concatenate([top, bottom], axis=1)


def polynomials(table_rows, quadrants, coef_table):
    a = jnp.take(coef_table, table_rows, axis=0)
    down = (quadrants // 2).astype(jnp.float32)[:, None, None]
    across = (quadrants % 2).astype(jnp.float32)[:, None]
    u = (jnp.arange(BLOCK).astype(jnp.float32)[None, :] + 0.5) / BLOCK - 1.0 + across
    u = u[:, None, :]
    q = a[:, :, 0, None] + u * (a[:, :, 1, None] + u * a[:, :, 3, None])
    s = a[:, :, 2, None] + u * a[:, :, 4, None]
    e = jnp.broadcast_to(a[:, :, 5, None], q.shape)
    poly = jnp.stack([q + down * (s + down * e), s + 2.0 * down * e, e], axis=2)
    return poly.transpose(1, 2, 0, 3)[:, :, :, None, :]


def window(image_ref, block, tile):
    start = TILE * tile - LEAD
    low, high = max(start, 0), min(start + WIN, BLOCK)
    part = image_ref[block, low:high, :]
    pieces = []
    if low > start:
        pieces.append(jnp.zeros((low - start, BLOCK), jnp.float32))
    pieces.append(part)
    if high < start + WIN:
        pieces.append(jnp.zeros((start + WIN - high, BLOCK), jnp.float32))
    return jnp.concatenate(pieces, axis=0) if len(pieces) > 1 else part


def matched_tile(tile, group, image_ref, left_ref, right_ref, poly_ref, parts_ref, emit):
    first = group * GROUP
    for pair in range(GROUP // 2):
        both = jnp.concatenate(
            [window(image_ref, first + 2 * pair, tile), window(image_ref, first + 2 * pair + 1, tile)], axis=1
        )
        high, low = split(both)
        rhs = jnp.concatenate([high, high, low, jnp.zeros((256 - 3 * WIN, 2 * BLOCK), jnp.bfloat16)], axis=0)
        spread = jnp.dot(left_ref[...], rhs, preferred_element_type=jnp.float32)
        for side in range(2):
            high, low = split(spread[:, side * BLOCK : (side + 1) * BLOCK])
            at = (2 * pair + side) * TILE
            parts_ref[:, at : at + TILE, :BLOCK] = high.reshape(NB, TILE, BLOCK)
            parts_ref[:, at : at + TILE, BLOCK:] = low.reshape(NB, TILE, BLOCK)
    t = (lax.broadcasted_iota(jnp.int32, (TILE, BLOCK), 0).astype(jnp.float32) + (TILE * tile + 0.5)) / BLOCK - 1.0
    total = [None] * GROUP
    for k in range(NB):
        both = jnp.dot(parts_ref[k], right_ref[k], preferred_element_type=jnp.float32)
        basis = both[:, :BLOCK] + both[:, BLOCK:]
        for block in range(GROUP):
            q = poly_ref[k, 0, first + block]
            s = poly_ref[k, 1, first + block]
            e = poly_ref[k, 2, first + block]
            term = (q + t * (s + t * e)) * basis[block * TILE : (block + 1) * TILE]
            total[block] = term if total[block] is None else total[block] + term
    for block in range(GROUP):
        emit(first + block, total[block])


def local_kernel(live_ref, image_ref, variance_ref, left_ref, right_ref, poly_ref, weighted_ref, inverse_ref, parts_ref):
    live = live_ref[0]

    def step(group, carry):
        for block in range(GROUP):
            at = group * GROUP + block
            flag = (at < live).astype(jnp.float32)
            inverse_ref[at] = flag / variance_ref[at]
        for tile in range(BLOCK // TILE):

            def emit(at, total, tile=tile):
                rows = slice(tile * TILE, (tile + 1) * TILE)
                weighted_ref[at, rows, :] = inverse_ref[at, rows, :] * total

            matched_tile(tile, group, image_ref, left_ref, right_ref, poly_ref, parts_ref, emit)
        return carry

    lax.fori_loop(0, image_ref.shape[0] // GROUP, step, 0)


def local_blocks(live, pixels, variances, left, right, poly):
    vmem = pl.BlockSpec(memory_space=pltpu.VMEM)
    return pl.pallas_call(
        local_kernel,
        out_shape=(jax.ShapeDtypeStruct(pixels.shape, jnp.float32),) * 2,
        in_specs=[pl.BlockSpec(memory_space=pltpu.SMEM)] + [vmem] * 5,
        out_specs=(vmem, vmem),
        scratch_shapes=[pltpu.VMEM((NB, GROUP * TILE, 2 * BLOCK), jnp.bfloat16)],
        compiler_params=pltpu.CompilerParams(vmem_limit_bytes=48 << 20),
        name="match_blocks",
    )(live, pixels, variances, left, right, poly)


def on_device(
    image, variance, dest_patch, quadrant, coef_index, block_count, coef_table, row_taps, col_taps
):
    pixels = image[0, 0]
    variances = variance[0, 0]
    targets = dest_patch[0, 0]
    quadrants = quadrant[0, 0]
    table_rows = coef_index[0, 0]
    live_count = block_count[0, 0]
    blocks = pixels.shape[0]
    block_side = pixels.shape[-1]
    left, right = bands(row_taps, col_taps)
    poly = polynomials(table_rows, quadrants, coef_table)
    weighted, inverse = local_blocks(block_count[0], pixels, variances, left, right, poly)
    owners = lax.axis_size("patch")
    capacity = 2
    slot_total = owners * capacity
    position = jnp.arange(blocks)
    is_live = position < live_count
    earlier_same = (targets[:, None] == targets[None, :]) & is_live[None, :] & (position[None, :] < position[:, None])
    slot_rank = jnp.sum(earlier_same.astype(jnp.int32), axis=1)
    slot_of = jnp.where(is_live, targets * capacity + slot_rank, -1)
    slot_match = slot_of[None, :] == jnp.arange(slot_total)[:, None]
    occupied = jnp.any(slot_match, axis=1)
    source = jnp.sum(slot_match.astype(jnp.int32) * position[None, :], axis=1)
    presence = occupied.astype(jnp.float32)
    quarter_hot = (quadrants[:, None] == jnp.arange(4)[None, :]).astype(jnp.float32)
    slot_quarter = (jnp.take(quarter_hot, source, axis=0) * presence[:, None]).reshape(owners, capacity, 4)
    grid_shape = (owners, capacity, block_side, block_side)
    slot_weighted = (jnp.take(weighted, source, axis=0) * presence[:, None, None]).reshape(grid_shape)
    slot_inverse = (jnp.take(inverse, source, axis=0) * presence[:, None, None]).reshape(grid_shape)
    send = functools.partial(lax.all_to_all, axis_name="patch", split_axis=0, concat_axis=0, tiled=True)
    got_quarter = send(slot_quarter).reshape(-1, 2, 2)
    patches = []
    for got in (send(slot_weighted), send(slot_inverse)):
        patch = jnp.einsum(
            "nab,nij->aibj", got_quarter, got.reshape(-1, block_side, block_side),
            precision=highest, preferred_element_type=jnp.float32,
        ).reshape(2 * block_side, 2 * block_side)
        patches.append(lax.psum_scatter(patch, "visit", scatter_dimension=0, tiled=True)[None])
    return tuple(patches)


def solution(mesh):
    placed = (
        P("visit", "patch", None, None, None),
        P("visit", "patch", None, None, None),
        P("visit", "patch", None),
        P("visit", "patch", None),
        P("visit", "patch", None),
        P("visit", "patch"),
        P(),
        P(),
        P(),
    )
    return jax.shard_map(
        on_device,
        mesh=mesh,
        in_specs=placed,
        out_specs=(P("patch", "visit", None), P("patch", "visit", None)),
        check_vma=False,
    )
```

```python
import functools
import itertools

import jax
import jax.numpy as jnp
from jax import lax
from jax.experimental import pallas as pl
from jax.experimental.pallas import tpu as pltpu
from jax.sharding import PartitionSpec as P

BLOCK = 128
TAPS = 41
REACH = TAPS // 2
NB = 16
BLOCKS = 32
TILE = 32
WIN = 80
LEAD = 24
GROUP = 8
STRIP = 8
SIDE = 4
SLOTS = 128
SLAB = BLOCKS * STRIP
MESH = pl.DeviceIdType.MESH
UNITS = ((0, 0, "x"), (0, 1, "z"), (1, 0, "y"), (1, 1, "y"))
AXES = ("x", "y", "z")


def split(x):
    high = x.astype(jnp.bfloat16)
    return high, (x - high.astype(jnp.float32)).astype(jnp.bfloat16)


def tap_rows(row_taps, col_taps):
    def parts(x):
        high = lax.reduce_precision(x, exponent_bits=8, mantissa_bits=7)
        return high, lax.reduce_precision(x - high, exponent_bits=8, mantissa_bits=7)

    def zeros(width):
        return jnp.zeros((NB, width), jnp.float32)

    high, low = parts(col_taps[:, ::-1])
    gap = zeros(WIN - TAPS)
    lead = LEAD - REACH
    row_high, row_low = parts(row_taps)
    around = zeros(BLOCK - TAPS)
    return jnp.concatenate(
        [
            zeros(lead), high, gap, low, gap, high, zeros(256 - 2 * WIN - lead - TAPS),
            row_high[:, REACH:], around, row_high[:, :REACH],
            row_low[:, REACH:], around, row_low[:, :REACH],
        ],
        axis=1,
    )


def build_bands(rows_ref, left_ref, right_ref):
    near = lax.broadcasted_iota(jnp.int32, (BLOCK, BLOCK), 1) - lax.broadcasted_iota(jnp.int32, (BLOCK, BLOCK), 0)
    near = (near <= REACH) & (near >= -REACH)

    def roll(row, height):
        return pltpu.roll(jnp.broadcast_to(row, (height, row.shape[1])), 0, 1, stride=1, stride_axis=0)

    for k in range(NB):
        band = roll(rows_ref[k : k + 1, :256], TILE)
        left_ref[k * TILE : (k + 1) * TILE, :] = band.astype(jnp.bfloat16)
        high = jnp.where(near, roll(rows_ref[k : k + 1, 256 : 256 + BLOCK], BLOCK), 0.0).astype(jnp.bfloat16)
        low = jnp.where(near, roll(rows_ref[k : k + 1, 256 + BLOCK :], BLOCK), 0.0).astype(jnp.bfloat16)
        right_ref[k, :BLOCK, :BLOCK] = high
        right_ref[k, :BLOCK, BLOCK:] = low
        right_ref[k, BLOCK:, :BLOCK] = high
        right_ref[k, BLOCK:, BLOCK:] = jnp.zeros_like(low)


def build_polynomials(coef_ref, quadrant_ref, poly_ref):
    column = lax.broadcasted_iota(jnp.int32, (NB, BLOCK), 1).astype(jnp.float32)
    own = (column + 0.5) / BLOCK - 1.0

    def build(b, carry):
        quadrant = quadrant_ref[b]
        down = (quadrant // 2).astype(jnp.float32)
        u = own + (quadrant % 2).astype(jnp.float32)
        a = coef_ref[b]
        a = [jnp.broadcast_to(a[:, m : m + 1], (NB, BLOCK)) for m in range(6)]
        q = a[0] + u * (a[1] + u * a[3])
        s = a[2] + u * a[4]
        e = a[5]
        poly_ref[b, 0] = q + down * (s + down * e)
        poly_ref[b, 1] = s + (2.0 * down) * e
        poly_ref[b, 2] = e
        return carry

    lax.fori_loop(0, BLOCKS, build, 0)


def window(image_ref, block, tile):
    start = TILE * tile - LEAD
    low, high = max(start, 0), min(start + WIN, BLOCK)
    part = image_ref[block, low:high, :]
    pieces = []
    if low > start:
        pieces.append(jnp.zeros((low - start, BLOCK), jnp.float32))
    pieces.append(part)
    if high < start + WIN:
        pieces.append(jnp.zeros((start + WIN - high, BLOCK), jnp.float32))
    return jnp.concatenate(pieces, axis=0) if len(pieces) > 1 else part


def matched_tile(tile, first, image_ref, left_ref, right_ref, poly_ref, parts_ref, emit):
    for pair in range(GROUP // 2):
        both = jnp.concatenate(
            [window(image_ref, first + 2 * pair, tile), window(image_ref, first + 2 * pair + 1, tile)], axis=1
        )
        high, low = split(both)
        rhs = jnp.concatenate([high, high, low, jnp.zeros((256 - 3 * WIN, 2 * BLOCK), jnp.bfloat16)], axis=0)
        spread = jnp.dot(left_ref[...], rhs, preferred_element_type=jnp.float32)
        for side in range(2):
            high, low = split(spread[:, side * BLOCK : (side + 1) * BLOCK])
            at = (2 * pair + side) * TILE
            parts_ref[:, at : at + TILE, :BLOCK] = high.reshape(NB, TILE, BLOCK)
            parts_ref[:, at : at + TILE, BLOCK:] = low.reshape(NB, TILE, BLOCK)
    t = (lax.broadcasted_iota(jnp.int32, (TILE, BLOCK), 0).astype(jnp.float32) + (TILE * tile + 0.5)) / BLOCK - 1.0
    total = [None] * GROUP
    for k in range(NB):
        both = jnp.dot(parts_ref[k], right_ref[k], preferred_element_type=jnp.float32)
        basis = both[:, :BLOCK] + both[:, BLOCK:]
        for block in range(GROUP):
            q = poly_ref[first + block, 0, k : k + 1, :]
            s = poly_ref[first + block, 1, k : k + 1, :]
            e = poly_ref[first + block, 2, k : k + 1, :]
            term = (q + t * (s + t * e)) * basis[block * TILE : (block + 1) * TILE]
            total[block] = term if total[block] is None else total[block] + term
    for block in range(GROUP):
        emit(first + block, total[block])


class Here:
    def __init__(self):
        self.y = lax.axis_index("visit")
        place = lax.axis_index("patch")
        self.x, self.z, self.c = lax.div(place, 8), lax.rem(lax.div(place, 2), 4), lax.rem(place, 2)
        self.odd = lax.rem(self.y + self.c, 2)

    def strip(self, axis):
        return getattr(self, axis) * 2 + self.c

    def at(self, c=0, **offsets):
        place = {axis: lax.rem(getattr(self, axis) + offsets.get(axis, 0), SIDE) for axis in AXES}
        place["c"] = lax.rem(self.c + c, 2)
        place["id"] = (place["y"], (place["x"] * SIDE + place["z"]) * 2 + place["c"])
        return place


def partners():
    found = set()
    for axis in AXES:
        others = [a for a in AXES if a != axis]
        for step, c in itertools.product(range(SIDE), range(2)):
            found.add(tuple(step if a == axis else 0 for a in AXES) + (c,))
        for steps in itertools.product(range(SIDE), repeat=2):
            to = dict(zip(others, steps))
            found.add(tuple(to.get(a, 0) for a in AXES) + (0,))
    found.discard((0, 0, 0, 0))
    return sorted(found)


def slot_rows(meta_ref, axis, here):
    patch, quadrant, live = meta_ref[0:1, :], meta_ref[1:2, :], meta_ref[2:3, :]
    x, z, c = lax.div(patch, 8), lax.rem(lax.div(patch, 2), 4), lax.rem(patch, 2)
    down, across = lax.div(quadrant, 2), lax.rem(quadrant, 2)
    if axis == "y":
        slot = (x * 4 + z) * 8 + c * 4 + down * 2 + across
    elif axis == "x":
        slot = (z * 2 + down) * 16 + (x * 2 + c) * 2 + across
    else:
        slot = (x * 2 + down) * 16 + (z * 2 + c) * 2 + across
    lane = lax.broadcasted_iota(jnp.int32, slot.shape, 1)
    mine = (lane >= here.strip(axis) * BLOCKS) & (lane < here.strip(axis) * BLOCKS + BLOCKS) & (live > 0)
    return jnp.broadcast_to(jnp.where(mine, slot, -1), (8, 256))


def fused_kernel(
    count_ref, quadrant_ref, image_ref, variance_ref, rows_ref, coef_ref, meta_ref, weighted_ref, weight_ref,
    left_ref, right_ref, poly_ref, parts_ref, strips_ref, slots_ref, got_slots_ref, got_ref, dense_ref, sums_y_ref, sums_ref,
    final_ref, got_final_ref,
    slots_send, slots_recv, first_send, first_recv, second_send, second_recv, third_send, third_recv,
):
    here = Here()
    barrier = pltpu.get_barrier_semaphore()
    all_partners = partners()
    for x, y, z, c in all_partners:
        pl.semaphore_signal(barrier, inc=1, device_id=here.at(x=x, y=y, z=z, c=c)["id"], device_id_type=MESH)

    live = count_ref[0]

    def invert(b, carry):
        flag = (b < live).astype(jnp.float32)
        rows = pl.ds(pl.multiple_of(b * STRIP, STRIP), STRIP)
        for chunk in range(BLOCK // STRIP):
            core, half, step = chunk // 8, chunk // 4 % 2, chunk % 4
            strips_ref[half * 8 + step * 2 + core, rows, :] = flag / variance_ref[b, chunk * STRIP : (chunk + 1) * STRIP, :]
        return carry

    lax.fori_loop(0, BLOCKS, invert, 0)
    for at, axis in enumerate(AXES):
        slots_ref[at] = slot_rows(meta_ref, axis, here)
    pl.semaphore_wait(barrier, len(all_partners))

    def remote(src, dst, send, recv, to):
        return pltpu.make_async_remote_copy(
            src_ref=src, dst_ref=dst, send_sem=send, recv_sem=recv, device_id=to["id"], device_id_type=MESH
        )

    def slots_copy(at, o):
        to = here.at(c=o % 2, **{AXES[at]: o // 2})
        return remote(slots_ref.at[at], got_slots_ref.at[at * 8 + o], slots_send.at[at, o], slots_recv.at[at, o], to)

    for at in range(3):
        for o in range(1, 8):
            slots_copy(at, o).start()

    def first_copy(unit, o, rows):
        axis = UNITS[unit][2]
        to = here.at(c=o % 2, **{axis: o // 2})
        source = strips_ref.at[unit * 8 + to[axis] * 2 + to["c"], rows, :]
        target = got_ref.at[unit * 8 + here.strip(axis), rows, :]
        if o == 0:
            return pltpu.make_async_copy(source, target, first_recv.at[unit, 0])
        return remote(source, target, first_send.at[unit, o], first_recv.at[unit, o], to)

    everything = pl.ds(0, SLAB)
    for unit in range(2):
        for o in range(8):
            first_copy(unit, o, everything).start()

    build_bands(rows_ref, left_ref, right_ref)
    build_polynomials(coef_ref, quadrant_ref, poly_ref)

    def compute(half):
        unit = 2 + half

        def step(group, carry):
            first = group * GROUP
            for core in range(2):

                def emit(b, total, core=core):
                    rows = pl.ds(pl.multiple_of(b * STRIP, STRIP), STRIP)
                    for step in range(SIDE):
                        at = step * 2 + core
                        strips_ref[unit * 8 + at, rows, :] = (
                            strips_ref[half * 8 + at, rows, :] * total[step * STRIP : (step + 1) * STRIP]
                        )

                matched_tile(core * 2 + half, first, image_ref, left_ref, right_ref, poly_ref, parts_ref, emit)
            rows = pl.ds(pl.multiple_of(group * GROUP * STRIP, GROUP * STRIP), GROUP * STRIP)
            for o in range(8):
                first_copy(unit, o, rows).start()
            return carry

        lax.fori_loop(0, BLOCKS // GROUP, step, 0)

    def take_slots(at):
        for o in range(1, 8):
            slots_copy(at, o).wait_recv()

    def second_copies(unit):
        axis = UNITS[unit][2]
        if axis == "y":
            for o in range(16):
                to = here.at(x=o // 4, z=o % 4)
                base = pl.multiple_of((to["x"] * SIDE + to["z"]) * 8, 8)
                yield o, to, dense_ref.at[unit, :, pl.ds(base, 8), :], sums_y_ref.at[unit - 2, o], o, o == 0
        else:
            other = "z" if axis == "x" else "x"
            for o in range(8):
                rise = here.odd + 2 * (o % 2)
                to = here.at(**{other: o // 2, "y": rise})
                base = pl.multiple_of((to[other] * 2 + lax.div(to["y"], 2)) * 16, 16)
                where = (o // 2) * 4 + rise
                yield o, to, dense_ref.at[unit, :, pl.ds(base, 16), :], sums_ref.at[unit, where], where, here.odd == 0 if o == 0 else False

    def start_second(unit):
        for o, to, source, target, where, own in second_copies(unit):
            away = remote(source, target, second_send.at[unit, o], second_recv.at[unit, where], to)
            home = pltpu.make_async_copy(source, target, second_recv.at[unit, where])
            if own is True:
                home.start()
            elif own is False:
                away.start()
            else:
                pl.when(own)(home.start)
                pl.when(jnp.logical_not(own))(away.start)

    def end_second(unit):
        for o, to, source, target, where, own in second_copies(unit):
            away = remote(source, target, second_send.at[unit, o], second_recv.at[unit, where], to)
            if own is True:
                continue
            if own is False:
                away.wait_send()
            else:
                pl.when(jnp.logical_not(own))(away.wait_send)

    def gather(unit):
        axis = UNITS[unit][2]
        for o in range(8):
            if o == 0:
                first_copy(unit, 0, everything).wait()
            else:
                first_copy(unit, o, everything).wait_recv()
        slots = slots_ref[AXES.index(axis)]
        for o in range(1, 8):
            slots = jnp.maximum(slots, got_slots_ref[AXES.index(axis) * 8 + o])
        hot = lax.broadcasted_iota(jnp.int32, (SLOTS, 256), 0) == slots[0:1, :]
        hot = hot.astype(jnp.float32).astype(jnp.bfloat16)
        for row in range(STRIP):
            data = jnp.concatenate(
                [got_ref[unit * 8 + o, pl.ds(row, BLOCKS, stride=STRIP), :] for o in range(8)], axis=0
            )
            both = jnp.dot(hot, jnp.concatenate(split(data), axis=1), preferred_element_type=jnp.float32)
            dense_ref[unit, row] = both[:, :BLOCK] + both[:, BLOCK:]
        start_second(unit)

    def third_copies(unit):
        axis = UNITS[unit][2]
        if axis == "y":
            for o in range(4):
                down, c = o // 2, o % 2
                to = here.at(c=c)
                owner = here.c + 2 * down
                to["id"] = (owner, to["id"][1])
                yield o, to, to["c"] * 2 + down, (owner == here.y if c == 0 else False)
        else:
            for o in range(8):
                to = here.at(c=o % 2, **{axis: o // 2})
                yield o, to, to[axis] * 2 + to["c"], o == 0

    def third_refs(unit, o, to, at):
        axis = UNITS[unit][2]
        source = final_ref.at[unit, pl.ds(pl.multiple_of(at * 16, 16), 16), :]
        where = getattr(here, axis)
        target = got_final_ref.at[unit, where]
        away = remote(source, target, third_send.at[unit, o], third_recv.at[unit, where], to)
        return away, pltpu.make_async_copy(source, target, third_recv.at[unit, where])

    def reduce(unit):
        axis = UNITS[unit][2]
        slots = 8 if axis == "y" else 16
        source = sums_y_ref.at[unit - 2] if axis == "y" else sums_ref.at[unit]

        def run():
            for o in range(16):
                pltpu.make_async_copy(source.at[o], source.at[o], second_recv.at[unit, o]).wait()
            for row in range(STRIP):
                total = source[0, row]
                for o in range(1, 16):
                    total = total + source[o, row]
                final_ref[unit, pl.ds(row, slots, stride=STRIP), :] = total
            for o, to, at, own in third_copies(unit):
                away, home = third_refs(unit, o, to, at)
                if own is True:
                    home.start()
                elif own is False:
                    away.start()
                else:
                    pl.when(own)(home.start)
                    pl.when(jnp.logical_not(own))(away.start)

        if axis == "y":
            run()
        else:
            pl.when(here.odd == 0)(run)

    def end_third(unit):
        def run():
            for o, to, at, own in third_copies(unit):
                away, _ = third_refs(unit, o, to, at)
                if own is True:
                    continue
                if own is False:
                    away.wait_send()
                else:
                    pl.when(jnp.logical_not(own))(away.wait_send)

        if UNITS[unit][2] == "y":
            run()
        else:
            pl.when(here.odd == 0)(run)

    def finish(unit):
        array, half, _ = UNITS[unit]
        out_ref = weighted_ref if array else weight_ref
        for step in range(SIDE):
            part = got_final_ref.at[unit, step]
            pltpu.make_async_copy(part, part, third_recv.at[unit, step]).wait()
            rows = slice(half * TILE + step * STRIP, half * TILE + (step + 1) * STRIP)
            out_ref[rows, :BLOCK] = got_final_ref[unit, step, :STRIP, :]
            out_ref[rows, BLOCK:] = got_final_ref[unit, step, STRIP:, :]

    compute(0)
    for at in range(3):
        take_slots(at)
    gather(0)
    gather(1)
    compute(1)
    gather(2)
    reduce(0)
    reduce(1)
    gather(3)
    reduce(2)
    finish(0)
    finish(1)
    reduce(3)
    finish(2)
    finish(3)
    for at in range(3):
        for o in range(1, 8):
            slots_copy(at, o).wait_send()
    for unit in range(4):
        for o in range(1, 8):
            first_copy(unit, o, everything).wait_send()
        end_second(unit)
        end_third(unit)


def fused(count, quadrants, pixels, variances, rows, coefs, meta):
    vmem = pl.BlockSpec(memory_space=pltpu.VMEM)
    smem = pl.BlockSpec(memory_space=pltpu.SMEM)
    dma = pltpu.SemaphoreType.DMA
    f32, bf16 = jnp.float32, jnp.bfloat16
    units = len(UNITS)
    return pl.pallas_call(
        fused_kernel,
        out_shape=(jax.ShapeDtypeStruct((64, 256), f32),) * 2,
        in_specs=[smem, smem] + [vmem] * 5,
        out_specs=(vmem, vmem),
        scratch_shapes=[
            pltpu.VMEM((NB * TILE, 256), bf16),
            pltpu.VMEM((NB, 256, 256), bf16),
            pltpu.VMEM((BLOCKS, 3, NB, BLOCK), f32),
            pltpu.VMEM((NB, GROUP * TILE, 256), bf16),
            pltpu.VMEM((units * 8, SLAB, BLOCK), f32),
            pltpu.VMEM((3, 8, 256), jnp.int32),
            pltpu.VMEM((24, 8, 256), jnp.int32),
            pltpu.VMEM((units * 8, SLAB, BLOCK), f32),
            pltpu.VMEM((units, STRIP, SLOTS, BLOCK), f32),
            pltpu.VMEM((2, 16, STRIP, 8, BLOCK), f32),
            pltpu.VMEM((2, 16, STRIP, 16, BLOCK), f32),
            pltpu.VMEM((units, 16 * STRIP, BLOCK), f32),
            pltpu.VMEM((units, SIDE, 2 * STRIP, BLOCK), f32),
            dma((3, 8)), dma((3, 8)),
            dma((units, 8)), dma((units, 8)),
            dma((units, 16)), dma((units, 16)),
            dma((units, 8)), dma((units, SIDE)),
        ],
        compiler_params=pltpu.CompilerParams(collective_id=0, has_side_effects=True, vmem_limit_bytes=56 << 20),
        name="coadd",
    )(count, quadrants, pixels, variances, rows, coefs, meta)


def on_device(
    image, variance, dest_patch, quadrant, coef_index, block_count, coef_table, row_taps, col_taps
):
    live = (jnp.arange(BLOCKS) < block_count[0, 0]).astype(jnp.int32)
    meta = jnp.stack([dest_patch[0, 0], quadrant[0, 0], live] + [live] * 5)
    meta = jnp.tile(meta, (1, 256 // BLOCKS))
    coefs = jnp.take(coef_table, coef_index[0, 0], axis=0)
    weighted, weight = fused(
        block_count[0], quadrant[0, 0], image[0, 0], variance[0, 0], tap_rows(row_taps, col_taps), coefs, meta
    )
    return weighted[None], weight[None]


def solution(mesh):
    placed = (
        P("visit", "patch", None, None, None),
        P("visit", "patch", None, None, None),
        P("visit", "patch", None),
        P("visit", "patch", None),
        P("visit", "patch", None),
        P("visit", "patch"),
        P(),
        P(),
        P(),
    )
    return jax.shard_map(
        on_device,
        mesh=mesh,
        in_specs=placed,
        out_specs=(P("patch", "visit", None), P("patch", "visit", None)),
        check_vma=False,
    )
```

```python
import itertools

import jax
import jax.numpy as jnp
from jax import lax
from jax.experimental import pallas as pl
from jax.experimental.pallas import tpu as pltpu
from jax.sharding import PartitionSpec as P

BLOCK = 128
TAPS = 41
REACH = TAPS // 2
NB = 16
BLOCKS = 32
TILE = 32
WIN = 80
LEAD = 24
GROUP = 8
STRIP = 8
SIDE = 4
SLOTS = 128
SLAB = BLOCKS * STRIP
MESH = pl.DeviceIdType.MESH
UNITS = ((0, 0, "x", "zy"), (0, 1, "z", "yx"), (1, 0, "y", "zx"), (1, 1, "x", "plane"))
AXES = ("x", "y", "z")


def split(x):
    high = x.astype(jnp.bfloat16)
    return high, (x - high.astype(jnp.float32)).astype(jnp.bfloat16)


def build_bands(row_ref, col_ref, left_ref, right_ref):
    tap = lax.broadcasted_iota(jnp.int32, (TAPS, 256), 0)
    lane = lax.broadcasted_iota(jnp.int32, (TAPS, 256), 1)

    def place(parts, *found):
        hot = [f.astype(jnp.float32).astype(jnp.bfloat16) for f in found]
        return sum(jnp.dot(p, h, preferred_element_type=jnp.float32) for p, h in zip(parts, hot))

    at = LEAD + REACH - tap
    spread_rows = place(split(col_ref[...]), (lane == at) | (lane == at + 2 * WIN), lane == at + WIN)
    at = lax.rem(tap + (BLOCK - REACH), BLOCK)
    high, low = split(row_ref[...])
    row_high, row_low = place((high,), lane == at)[:, :BLOCK], place((low,), lane == at)[:, :BLOCK]
    near = lax.broadcasted_iota(jnp.int32, (BLOCK, BLOCK), 1) - lax.broadcasted_iota(jnp.int32, (BLOCK, BLOCK), 0)
    near = (near <= REACH) & (near >= -REACH)

    def roll(row, height):
        return pltpu.roll(jnp.broadcast_to(row, (height, row.shape[1])), 0, 1, stride=1, stride_axis=0)

    for k in range(NB):
        band = roll(spread_rows[k : k + 1, :], TILE)
        left_ref[k * TILE : (k + 1) * TILE, :] = band.astype(jnp.bfloat16)
        high = jnp.where(near, roll(row_high[k : k + 1, :], BLOCK), 0.0).astype(jnp.bfloat16)
        low = jnp.where(near, roll(row_low[k : k + 1, :], BLOCK), 0.0).astype(jnp.bfloat16)
        right_ref[k, :BLOCK, :BLOCK] = high
        right_ref[k, :BLOCK, BLOCK:] = low
        right_ref[k, BLOCK:, :BLOCK] = high
        right_ref[k, BLOCK:, BLOCK:] = jnp.zeros_like(low)


def build_polynomials(table_ref, index_ref, quadrant_ref, poly_ref):
    entry = lax.broadcasted_iota(jnp.int32, (table_ref.shape[1], BLOCK), 0)
    index = jnp.concatenate([index_ref[...]] * (BLOCK // BLOCKS), axis=1)
    hot = (entry == index).astype(jnp.float32).astype(jnp.bfloat16)
    rest, coefs = table_ref[...], None
    for _ in range(3):
        part = rest.astype(jnp.bfloat16)
        rest = rest - part.astype(jnp.float32)
        picked = jnp.dot(part, hot, preferred_element_type=jnp.float32)
        coefs = picked if coefs is None else coefs + picked
    column = lax.broadcasted_iota(jnp.int32, (NB, BLOCK), 1).astype(jnp.float32)
    own = (column + 0.5) / BLOCK - 1.0
    for b in range(BLOCKS):
        quadrant = quadrant_ref[b]
        down = (quadrant // 2).astype(jnp.float32)
        u = own + (quadrant % 2).astype(jnp.float32)
        a = [jnp.broadcast_to(coefs[m * NB : (m + 1) * NB, b : b + 1], (NB, BLOCK)) for m in range(6)]
        q = a[0] + u * (a[1] + u * a[3])
        s = a[2] + u * a[4]
        e = a[5]
        poly_ref[b, 0] = q + down * (s + down * e)
        poly_ref[b, 1] = s + (2.0 * down) * e
        poly_ref[b, 2] = e


def window(image_ref, block, tile):
    start = TILE * tile - LEAD
    low, high = max(start, 0), min(start + WIN, BLOCK)
    part = image_ref[block, low:high, :]
    pieces = []
    if low > start:
        pieces.append(jnp.zeros((low - start, BLOCK), jnp.float32))
    pieces.append(part)
    if high < start + WIN:
        pieces.append(jnp.zeros((start + WIN - high, BLOCK), jnp.float32))
    return jnp.concatenate(pieces, axis=0) if len(pieces) > 1 else part


def matched_tile(tile, first, image_ref, left_ref, right_ref, poly_ref, parts_ref, emit):
    for pair in range(GROUP // 2):
        both = jnp.concatenate(
            [window(image_ref, first + 2 * pair, tile), window(image_ref, first + 2 * pair + 1, tile)], axis=1
        )
        high, low = split(both)
        rhs = jnp.concatenate([high, high, low, jnp.zeros((256 - 3 * WIN, 2 * BLOCK), jnp.bfloat16)], axis=0)
        spread = jnp.dot(left_ref[...], rhs, preferred_element_type=jnp.float32)
        for side in range(2):
            high, low = split(spread[:, side * BLOCK : (side + 1) * BLOCK])
            at = (2 * pair + side) * TILE
            parts_ref[:, at : at + TILE, :BLOCK] = high.reshape(NB, TILE, BLOCK)
            parts_ref[:, at : at + TILE, BLOCK:] = low.reshape(NB, TILE, BLOCK)
    t = (lax.broadcasted_iota(jnp.int32, (TILE, BLOCK), 0).astype(jnp.float32) + (TILE * tile + 0.5)) / BLOCK - 1.0
    total = [None] * GROUP
    for k in range(NB):
        both = jnp.dot(parts_ref[k], right_ref[k], preferred_element_type=jnp.float32)
        basis = both[:, :BLOCK] + both[:, BLOCK:]
        for block in range(GROUP):
            q = poly_ref[first + block, 0, k : k + 1, :]
            s = poly_ref[first + block, 1, k : k + 1, :]
            e = poly_ref[first + block, 2, k : k + 1, :]
            term = (q + t * (s + t * e)) * basis[block * TILE : (block + 1) * TILE]
            total[block] = term if total[block] is None else total[block] + term
    for block in range(GROUP):
        emit(first + block, total[block])


class Here:
    def __init__(self):
        self.y = lax.axis_index("visit")
        place = lax.axis_index("patch")
        self.x, self.z, self.c = lax.div(place, 8), lax.rem(lax.div(place, 2), 4), lax.rem(place, 2)
        self.odd = lax.rem(self.y + self.c, 2)

    def strip(self, axis):
        return getattr(self, axis) * 2 + self.c

    def at(self, c=0, **offsets):
        place = {axis: lax.rem(getattr(self, axis) + offsets.get(axis, 0), SIDE) for axis in AXES}
        place["c"] = lax.rem(self.c + c, 2)
        place["id"] = (place["y"], (place["x"] * SIDE + place["z"]) * 2 + place["c"])
        return place


def partners():
    found = set()
    for axis in AXES:
        others = [a for a in AXES if a != axis]
        for step, c in itertools.product(range(SIDE), range(2)):
            found.add(tuple(step if a == axis else 0 for a in AXES) + (c,))
        for steps in itertools.product(range(SIDE), repeat=2):
            to = dict(zip(others, steps))
            found.add(tuple(to.get(a, 0) for a in AXES) + (0,))
    found.discard((0, 0, 0, 0))
    return sorted(found)


def slot_rows(patches, quadrants, live, unit, here):
    _, _, axis, later = UNITS[unit]
    patch, quadrant = (jnp.concatenate([ref[...]] * 8, axis=1) for ref in (patches, quadrants))
    part = {"x": lax.div(patch, 8), "z": lax.rem(lax.div(patch, 2), 4)}
    sizes = {"x": 4, "z": 4, "y": 2}
    c = lax.rem(patch, 2)
    down, across = lax.div(quadrant, 2), lax.rem(quadrant, 2)
    part["y"] = down
    order = later if later != "plane" else "".join(a for a in "xzy" if a != axis)
    slot = part[order[0]] * sizes[order[1]] + part[order[1]]
    if axis == "y":
        slot = slot * 8 + c * 4 + down * 2 + across
    else:
        slot = slot * 16 + part[axis] * 4 + c * 2 + across
    lane = lax.broadcasted_iota(jnp.int32, slot.shape, 1)
    at = lane - here.strip(axis) * BLOCKS
    mine = (at >= 0) & (at < jnp.minimum(live, BLOCKS))
    return jnp.broadcast_to(jnp.where(mine, slot, -1), (8, 256))


def fused_kernel(
    count_ref, quadrant_ref, image_ref, variance_ref, row_ref, col_ref, table_ref, index_ref, patches_ref, quadrants_ref,
    out_ref,
    left_ref, right_ref, poly_ref, parts_ref, strips_ref, slots_ref, got_slots_ref, got_ref, dense_ref, near_ref, middle_ref, far_ref, sums_ref,
    final_ref, got_final_ref,
    slots_send, slots_recv, first_send, first_recv, second_send, second_recv, third_send, third_recv,
):
    here = Here()
    barrier = pltpu.get_barrier_semaphore()
    all_partners = partners()
    for x, y, z, c in all_partners:
        pl.semaphore_signal(barrier, inc=1, device_id=here.at(x=x, y=y, z=z, c=c)["id"], device_id_type=MESH)

    live = count_ref[0]

    def invert(b, carry):
        flag = (b < live).astype(jnp.float32)
        rows = pl.ds(pl.multiple_of(b * STRIP, STRIP), STRIP)
        for chunk in range(BLOCK // STRIP):
            core, half, step = chunk // 8, chunk // 4 % 2, chunk % 4
            strips_ref[half * 8 + step * 2 + core, rows, :] = flag / variance_ref[b, chunk * STRIP : (chunk + 1) * STRIP, :]
        return carry

    lax.fori_loop(0, BLOCKS, invert, 0)
    for unit in range(4):
        slots_ref[unit] = slot_rows(patches_ref, quadrants_ref, live, unit, here)
    pl.semaphore_wait(barrier, len(all_partners))

    def remote(src, dst, send, recv, to):
        return pltpu.make_async_remote_copy(
            src_ref=src, dst_ref=dst, send_sem=send, recv_sem=recv, device_id=to["id"], device_id_type=MESH
        )

    def slots_copy(unit, o):
        to = here.at(c=o % 2, **{UNITS[unit][2]: o // 2})
        return remote(slots_ref.at[unit], got_slots_ref.at[unit * 8 + o], slots_send.at[unit, o], slots_recv.at[unit, o], to)

    def first_copy(unit, o, rows):
        axis = UNITS[unit][2]
        to = here.at(c=o % 2, **{axis: o // 2})
        source = strips_ref.at[unit * 8 + to[axis] * 2 + to["c"], rows, :]
        target = got_ref.at[unit * 8 + here.strip(axis), rows, :]
        if o == 0:
            return pltpu.make_async_copy(source, target, first_recv.at[unit, 0])
        return remote(source, target, first_send.at[unit, o], first_recv.at[unit, o], to)

    everything = pl.ds(0, SLAB)
    for unit in range(2):
        for o in range(8):
            first_copy(unit, o, everything).start()
    for unit in range(4):
        for o in range(1, 8):
            slots_copy(unit, o).start()

    build_bands(row_ref, col_ref, left_ref, right_ref)
    build_polynomials(table_ref, index_ref, quadrant_ref, poly_ref)

    def compute(half, begin, end):
        unit = 2 + half

        def step(group, carry):
            first = group * GROUP
            for core in range(2):

                def emit(b, total, core=core):
                    rows = pl.ds(pl.multiple_of(b * STRIP, STRIP), STRIP)
                    for step in range(SIDE):
                        at = step * 2 + core
                        strips_ref[unit * 8 + at, rows, :] = (
                            strips_ref[half * 8 + at, rows, :] * total[step * STRIP : (step + 1) * STRIP]
                        )

                matched_tile(core * 2 + half, first, image_ref, left_ref, right_ref, poly_ref, parts_ref, emit)
            rows = pl.ds(pl.multiple_of(group * GROUP * STRIP, GROUP * STRIP), GROUP * STRIP)
            for o in range(8):
                first_copy(unit, o, rows).start()
            return carry

        lax.fori_loop(begin, end, step, 0)

    def take_slots(unit):
        for o in range(1, 8):
            slots_copy(unit, o).wait_recv()

    def choose(own, home, away):
        if own is True:
            home()
        elif own is False:
            away()
        else:
            pl.when(own)(home)
            pl.when(jnp.logical_not(own))(away)

    def nothing():
        pass

    def halved(unit, axis):
        return axis == "y" and UNITS[unit][2] != "y"

    def steps(unit, axis):
        if halved(unit, axis):
            for m in range(2):
                rise = here.odd + 2 * m
                to = here.at(y=rise)
                yield rise, to, lax.div(to["y"], 2), (here.odd == 0 if m == 0 else False)
        else:
            for o in range(SIDE):
                to = here.at(**{axis: o})
                yield o, to, to[axis], o == 0

    def width(unit):
        return 8 if UNITS[unit][2] == "y" else 16

    def line(unit, second):
        axis = UNITS[unit][3][second]
        slots = width(unit)
        if not second:
            slots = slots * (2 if halved(unit, UNITS[unit][3][1]) else SIDE)
        source, target = (middle_ref, far_ref) if second else (dense_ref, near_ref)
        for at, (o, to, share, own) in enumerate(steps(unit, axis)):
            part = source.at[unit, :, pl.ds(pl.multiple_of(share * slots, 8), slots), :]
            place = target.at[unit, o, :, pl.ds(0, slots), :]
            arrived = second_recv.at[unit, 4 * second + o]
            yield (
                pltpu.make_async_copy(part, place, arrived) if own is not False else None,
                remote(part, place, second_send.at[unit, 4 * second + at], arrived, to) if own is not True else None,
                own,
            )

    def plane(unit):
        slots = width(unit)
        first, last = (a for a in "xzy" if a != UNITS[unit][2])
        for at, ((o, to, share, own), (p, on, more, also)) in enumerate(
            itertools.product(steps(unit, first), steps(unit, last))
        ):
            to = dict(to, **{last: on[last]})
            to["id"] = (to["y"], (to["x"] * SIDE + to["z"]) * 2 + to["c"])
            base = pl.multiple_of((share * (2 if halved(unit, last) else SIDE) + more) * slots, 8)
            part = dense_ref.at[unit, :, pl.ds(base, slots), :]
            place = sums_ref.at[o * SIDE + p, :, pl.ds(0, slots), :]
            arrived = second_recv.at[unit, o * SIDE + p]
            own = False if own is False or also is False else also if own is True else own
            yield (
                pltpu.make_async_copy(part, place, arrived) if own is not False else None,
                remote(part, place, second_send.at[unit, at], arrived, to) if own is not True else None,
                own,
            )

    def start_all(copies):
        for home, away, own in copies:
            choose(own, home and home.start, away and away.start)

    def end_all(copies):
        for home, away, own in copies:
            choose(own, nothing, away and away.wait_send)

    def start_second(unit):
        start_all(plane(unit) if UNITS[unit][3] == "plane" else line(unit, 0))

    def arrived_sum(source, slots, unit, sems):
        for n, at in enumerate(sems):
            part = source.at[n, :, pl.ds(0, slots), :]
            pltpu.make_async_copy(part, part, second_recv.at[unit, at]).wait()

    def where_owner(unit, axis, run):
        if halved(unit, axis):
            pl.when(here.odd == 0)(run)
        else:
            run()

    def pass_on(unit):
        first, last = UNITS[unit][3]
        slots = width(unit) * (2 if halved(unit, last) else SIDE)

        def run():
            arrived_sum(near_ref.at[unit], slots, unit, range(4))
            for row in range(STRIP):
                total = near_ref[unit, 0, row, :slots, :]
                for o in range(1, SIDE):
                    total = total + near_ref[unit, o, row, :slots, :]
                middle_ref[unit, row, :slots, :] = total
            start_all(line(unit, 1))

        where_owner(unit, first, run)

    def end_second(unit):
        if UNITS[unit][3] == "plane":
            end_all(plane(unit))
        else:
            end_all(line(unit, 0))
            where_owner(unit, UNITS[unit][3][0], lambda: end_all(line(unit, 1)))

    def gather(unit):
        for o in range(8):
            if o == 0:
                first_copy(unit, 0, everything).wait()
            else:
                first_copy(unit, o, everything).wait_recv()
        take_slots(unit)
        slots = slots_ref[unit]
        for o in range(1, 8):
            slots = jnp.maximum(slots, got_slots_ref[unit * 8 + o])
        hot = lax.broadcasted_iota(jnp.int32, (SLOTS, 256), 0) == slots[0:1, :]
        hot = hot.astype(jnp.float32).astype(jnp.bfloat16)
        for row in range(STRIP):
            data = jnp.concatenate(
                [got_ref[unit * 8 + o, pl.ds(row, BLOCKS, stride=STRIP), :] for o in range(8)], axis=0
            )
            both = jnp.dot(hot, jnp.concatenate(split(data), axis=1), preferred_element_type=jnp.float32)
            dense_ref[unit, row] = both[:, :BLOCK] + both[:, BLOCK:]
        start_second(unit)

    def third_copies(unit):
        axis = UNITS[unit][2]
        if axis == "y":
            for o in range(4):
                down, c = o // 2, o % 2
                to = here.at(c=c)
                owner = here.c + 2 * down
                to["id"] = (owner, to["id"][1])
                yield o, to, to["c"] * 2 + down, (owner == here.y if c == 0 else False)
        else:
            for o in range(8):
                to = here.at(c=o % 2, **{axis: o // 2})
                yield o, to, to[axis] * 2 + to["c"], o == 0

    def third_refs(unit, o, to, at):
        axis = UNITS[unit][2]
        source = final_ref.at[unit, pl.ds(pl.multiple_of(at * 16, 16), 16), :]
        where = getattr(here, axis)
        target = got_final_ref.at[unit, where]
        away = remote(source, target, third_send.at[unit, o], third_recv.at[unit, where], to)
        return away, pltpu.make_async_copy(source, target, third_recv.at[unit, where])

    def reduce(unit):
        axis = UNITS[unit][2]
        slots = width(unit)

        def run():
            if UNITS[unit][3] == "plane":
                source, sems = sums_ref, range(16)
            else:
                source, sems = far_ref.at[unit], range(4, 8)
            arrived_sum(source, slots, unit, sems)
            for row in range(STRIP):
                total = source[0, row, :slots, :]
                for o in range(1, len(sems)):
                    total = total + source[o, row, :slots, :]
                final_ref[unit, pl.ds(row, slots, stride=STRIP), :] = total
            for o, to, at, own in third_copies(unit):
                away, home = third_refs(unit, o, to, at)
                if own is True:
                    home.start()
                elif own is False:
                    away.start()
                else:
                    pl.when(own)(home.start)
                    pl.when(jnp.logical_not(own))(away.start)

        if axis == "y":
            run()
        else:
            pl.when(here.odd == 0)(run)

    def end_third(unit):
        def run():
            for o, to, at, own in third_copies(unit):
                away, _ = third_refs(unit, o, to, at)
                if own is True:
                    continue
                if own is False:
                    away.wait_send()
                else:
                    pl.when(jnp.logical_not(own))(away.wait_send)

        if UNITS[unit][2] == "y":
            run()
        else:
            pl.when(here.odd == 0)(run)

    def finish(unit):
        array, half = UNITS[unit][:2]
        for step in range(SIDE):
            part = got_final_ref.at[unit, step]
            pltpu.make_async_copy(part, part, third_recv.at[unit, step]).wait()
            rows = slice(half * TILE + step * STRIP, half * TILE + (step + 1) * STRIP)
            out_ref[array, rows, :BLOCK] = got_final_ref[unit, step, :STRIP, :]
            out_ref[array, rows, BLOCK:] = got_final_ref[unit, step, STRIP:, :]

    compute(0, 0, 4)
    gather(0)
    gather(1)
    compute(1, 0, 2)
    pass_on(0)
    pass_on(1)
    gather(2)
    compute(1, 2, 4)
    pass_on(2)
    reduce(0)
    reduce(1)
    gather(3)
    reduce(2)
    finish(0)
    finish(1)
    finish(2)
    reduce(3)
    finish(3)
    for unit in range(4):
        for o in range(1, 8):
            slots_copy(unit, o).wait_send()
        for o in range(1, 8):
            first_copy(unit, o, everything).wait_send()
        end_second(unit)
        end_third(unit)


def fused(count, quadrants, *arrays):
    vmem = pl.BlockSpec(memory_space=pltpu.VMEM)
    smem = pl.BlockSpec(memory_space=pltpu.SMEM)
    dma = pltpu.SemaphoreType.DMA
    f32, bf16 = jnp.float32, jnp.bfloat16
    units = len(UNITS)
    return pl.pallas_call(
        fused_kernel,
        out_shape=jax.ShapeDtypeStruct((2, 64, 256), f32),
        in_specs=[smem, smem] + [vmem] * len(arrays),
        out_specs=vmem,
        scratch_shapes=[
            pltpu.VMEM((NB * TILE, 256), bf16),
            pltpu.VMEM((NB, 256, 256), bf16),
            pltpu.VMEM((BLOCKS, 3, NB, BLOCK), f32),
            pltpu.VMEM((NB, GROUP * TILE, 256), bf16),
            pltpu.VMEM((units * 8, SLAB, BLOCK), f32),
            pltpu.VMEM((units, 8, 256), jnp.int32),
            pltpu.VMEM((units * 8, 8, 256), jnp.int32),
            pltpu.VMEM((units * 8, SLAB, BLOCK), f32),
            pltpu.VMEM((units, STRIP, SLOTS, BLOCK), f32),
            pltpu.VMEM((units, SIDE, STRIP, 64, BLOCK), f32),
            pltpu.VMEM((units, STRIP, 64, BLOCK), f32),
            pltpu.VMEM((units, SIDE, STRIP, 16, BLOCK), f32),
            pltpu.VMEM((16, STRIP, 16, BLOCK), f32),
            pltpu.VMEM((units, 16 * STRIP, BLOCK), f32),
            pltpu.VMEM((units, SIDE, 2 * STRIP, BLOCK), f32),
            dma((units, 8)), dma((units, 8)),
            dma((units, 8)), dma((units, 8)),
            dma((units, 16)), dma((units, 16)),
            dma((units, 8)), dma((units, SIDE)),
        ],
        compiler_params=pltpu.CompilerParams(collective_id=0, has_side_effects=True, vmem_limit_bytes=56 << 20),
        name="coadd",
    )(count, quadrants, *arrays)


def on_device(
    image, variance, dest_patch, quadrant, coef_index, block_count, coef_table, row_taps, col_taps
):
    table = coef_table.transpose(2, 1, 0).reshape(-1, coef_table.shape[0])
    sums = fused(
        block_count[0], quadrant[0, 0], image[0, 0], variance[0, 0], row_taps, col_taps, table,
        coef_index[0], dest_patch[0], quadrant[0],
    )
    return sums[1][None], sums[0][None]


def solution(mesh):
    placed = (
        P("visit", "patch", None, None, None),
        P("visit", "patch", None, None, None),
        P("visit", "patch", None),
        P("visit", "patch", None),
        P("visit", "patch", None),
        P("visit", "patch"),
        P(),
        P(),
        P(),
    )
    return jax.shard_map(
        on_device,
        mesh=mesh,
        in_specs=placed,
        out_specs=(P("patch", "visit", None), P("patch", "visit", None)),
        check_vma=False,
    )
```

```python
import itertools

import jax
import jax.numpy as jnp
from jax import lax
from jax.experimental import pallas as pl
from jax.experimental.pallas import tpu as pltpu
from jax.sharding import PartitionSpec as P

BLOCK = 128
TAPS = 41
REACH = TAPS // 2
NB = 16
BLOCKS = 32
TILE = 32
WIN = 80
LEAD = 24
GROUP = 8
STRIP = 8
SIDE = 4
SLOTS = 128
SLAB = BLOCKS * STRIP
MESH = pl.DeviceIdType.MESH
UNITS = ((0, 0, "x", "zy"), (0, 1, "z", "yx"), (1, 0, "y", "zx"), (1, 1, "x", "plane"))
AXES = ("x", "y", "z")


def split(x):
    high = x.astype(jnp.bfloat16)
    return high, (x - high.astype(jnp.float32)).astype(jnp.bfloat16)


def build_bands(row_ref, col_ref, left_ref, right_ref):
    tap = lax.broadcasted_iota(jnp.int32, (TAPS, 256), 0)
    lane = lax.broadcasted_iota(jnp.int32, (TAPS, 256), 1)

    def place(parts, *found):
        hot = [f.astype(jnp.float32).astype(jnp.bfloat16) for f in found]
        return sum(jnp.dot(p, h, preferred_element_type=jnp.float32) for p, h in zip(parts, hot))

    at = LEAD + REACH - tap
    spread_rows = place(split(col_ref[...]), (lane == at) | (lane == at + 2 * WIN), lane == at + WIN)
    at = lax.rem(tap + (BLOCK - REACH), BLOCK)
    high, low = split(row_ref[...])
    row_high, row_low = place((high,), lane == at)[:, :BLOCK], place((low,), lane == at)[:, :BLOCK]
    near = lax.broadcasted_iota(jnp.int32, (BLOCK, BLOCK), 1) - lax.broadcasted_iota(jnp.int32, (BLOCK, BLOCK), 0)
    near = (near <= REACH) & (near >= -REACH)

    def roll(row, height):
        return pltpu.roll(jnp.broadcast_to(row, (height, row.shape[1])), 0, 1, stride=1, stride_axis=0)

    for k in range(NB):
        band = roll(spread_rows[k : k + 1, :], TILE)
        left_ref[k * TILE : (k + 1) * TILE, :] = band.astype(jnp.bfloat16)
        high = jnp.where(near, roll(row_high[k : k + 1, :], BLOCK), 0.0).astype(jnp.bfloat16)
        low = jnp.where(near, roll(row_low[k : k + 1, :], BLOCK), 0.0).astype(jnp.bfloat16)
        right_ref[k, :BLOCK, :BLOCK] = high
        right_ref[k, :BLOCK, BLOCK:] = low
        right_ref[k, BLOCK:, :BLOCK] = high
        right_ref[k, BLOCK:, BLOCK:] = jnp.zeros_like(low)


def build_polynomials(table_ref, index_ref, quadrant_ref, poly_ref):
    entry = lax.broadcasted_iota(jnp.int32, (table_ref.shape[1], BLOCK), 0)
    index = jnp.concatenate([index_ref[...]] * (BLOCK // BLOCKS), axis=1)
    hot = (entry == index).astype(jnp.float32).astype(jnp.bfloat16)
    rest, coefs = table_ref[...], None
    for _ in range(3):
        part = rest.astype(jnp.bfloat16)
        rest = rest - part.astype(jnp.float32)
        picked = jnp.dot(part, hot, preferred_element_type=jnp.float32)
        coefs = picked if coefs is None else coefs + picked
    column = lax.broadcasted_iota(jnp.int32, (NB, BLOCK), 1).astype(jnp.float32)
    own = (column + 0.5) / BLOCK - 1.0
    for b in range(BLOCKS):
        quadrant = quadrant_ref[b]
        down = (quadrant // 2).astype(jnp.float32)
        u = own + (quadrant % 2).astype(jnp.float32)
        a = [jnp.broadcast_to(coefs[m * NB : (m + 1) * NB, b : b + 1], (NB, BLOCK)) for m in range(6)]
        q = a[0] + u * (a[1] + u * a[3])
        s = a[2] + u * a[4]
        e = a[5]
        poly_ref[b, 0] = q + down * (s + down * e)
        poly_ref[b, 1] = s + (2.0 * down) * e
        poly_ref[b, 2] = e


def window(image_ref, block, tile):
    start = TILE * tile - LEAD
    low, high = max(start, 0), min(start + WIN, BLOCK)
    part = image_ref[block, low:high, :]
    pieces = []
    if low > start:
        pieces.append(jnp.zeros((low - start, BLOCK), jnp.float32))
    pieces.append(part)
    if high < start + WIN:
        pieces.append(jnp.zeros((start + WIN - high, BLOCK), jnp.float32))
    return jnp.concatenate(pieces, axis=0) if len(pieces) > 1 else part


def matched_tile(tile, first, image_ref, left_ref, right_ref, poly_ref, parts_ref, emit):
    for pair in range(GROUP // 2):
        both = jnp.concatenate(
            [window(image_ref, first + 2 * pair, tile), window(image_ref, first + 2 * pair + 1, tile)], axis=1
        )
        high, low = split(both)
        rhs = jnp.concatenate([high, high, low, jnp.zeros((256 - 3 * WIN, 2 * BLOCK), jnp.bfloat16)], axis=0)
        spread = jnp.dot(left_ref[...], rhs, preferred_element_type=jnp.float32)
        for side in range(2):
            high, low = split(spread[:, side * BLOCK : (side + 1) * BLOCK])
            at = (2 * pair + side) * TILE
            parts_ref[:, at : at + TILE, :BLOCK] = high.reshape(NB, TILE, BLOCK)
            parts_ref[:, at : at + TILE, BLOCK:] = low.reshape(NB, TILE, BLOCK)
    t = (lax.broadcasted_iota(jnp.int32, (TILE, BLOCK), 0).astype(jnp.float32) + (TILE * tile + 0.5)) / BLOCK - 1.0
    total = [None] * GROUP
    for k in range(NB):
        both = jnp.dot(parts_ref[k], right_ref[k], preferred_element_type=jnp.float32)
        basis = both[:, :BLOCK] + both[:, BLOCK:]
        for block in range(GROUP):
            q = poly_ref[first + block, 0, k : k + 1, :]
            s = poly_ref[first + block, 1, k : k + 1, :]
            e = poly_ref[first + block, 2, k : k + 1, :]
            term = (q + t * (s + t * e)) * basis[block * TILE : (block + 1) * TILE]
            total[block] = term if total[block] is None else total[block] + term
    for block in range(GROUP):
        emit(first + block, total[block])


class Here:
    def __init__(self):
        self.y = lax.axis_index("visit")
        place = lax.axis_index("patch")
        self.x, self.z, self.c = lax.div(place, 8), lax.rem(lax.div(place, 2), 4), lax.rem(place, 2)
        self.odd = lax.rem(self.y + self.c, 2)

    def strip(self, axis):
        return getattr(self, axis) * 2 + self.c

    def at(self, c=0, **offsets):
        place = {axis: lax.rem(getattr(self, axis) + offsets.get(axis, 0), SIDE) for axis in AXES}
        place["c"] = lax.rem(self.c + c, 2)
        place["id"] = (place["y"], (place["x"] * SIDE + place["z"]) * 2 + place["c"])
        return place


def partners():
    found = set()
    for axis in AXES:
        others = [a for a in AXES if a != axis]
        for step, c in itertools.product(range(SIDE), range(2)):
            found.add(tuple(step if a == axis else 0 for a in AXES) + (c,))
        for steps in itertools.product(range(SIDE), repeat=2):
            to = dict(zip(others, steps))
            found.add(tuple(to.get(a, 0) for a in AXES) + (0,))
    found.discard((0, 0, 0, 0))
    return sorted(found)


def slot_rows(patches, quadrants, live, unit, here):
    _, _, axis, later = UNITS[unit]
    patch, quadrant = (jnp.concatenate([ref[...]] * 8, axis=1) for ref in (patches, quadrants))
    part = {"x": lax.div(patch, 8), "z": lax.rem(lax.div(patch, 2), 4)}
    sizes = {"x": 4, "z": 4, "y": 2}
    c = lax.rem(patch, 2)
    down, across = lax.div(quadrant, 2), lax.rem(quadrant, 2)
    part["y"] = down
    order = later if later != "plane" else "".join(a for a in "xzy" if a != axis)
    slot = part[order[0]] * sizes[order[1]] + part[order[1]]
    if axis == "y":
        slot = slot * 8 + c * 4 + down * 2 + across
    else:
        slot = slot * 16 + part[axis] * 4 + c * 2 + across
    lane = lax.broadcasted_iota(jnp.int32, slot.shape, 1)
    at = lane - here.strip(axis) * BLOCKS
    mine = (at >= 0) & (at < jnp.minimum(live, BLOCKS))
    return jnp.broadcast_to(jnp.where(mine, slot, -1), (8, 256))


def fused_kernel(
    count_ref, quadrant_ref, image_hbm, variance_hbm, row_ref, col_ref, table_ref, index_ref, patches_ref, quadrants_ref,
    out_ref,
    image_ref, variance_ref, load_sem, left_ref, right_ref, poly_ref, parts_ref, strips_ref, slots_ref, got_slots_ref, got_ref, dense_ref, near_ref, middle_ref, far_ref, sums_ref,
    final_ref, got_final_ref,
    slots_send, slots_recv, first_send, first_recv, second_send, second_recv, third_send, third_recv,
):
    here = Here()
    barrier = pltpu.get_barrier_semaphore()
    all_partners = partners()
    for x, y, z, c in all_partners:
        pl.semaphore_signal(barrier, inc=1, device_id=here.at(x=x, y=y, z=z, c=c)["id"], device_id_type=MESH)

    load_variance = pltpu.make_async_copy(variance_hbm, variance_ref, load_sem.at[0])
    load_image = pltpu.make_async_copy(image_hbm, image_ref, load_sem.at[1])
    load_variance.start()
    load_image.start()
    build_bands(row_ref, col_ref, left_ref, right_ref)
    build_polynomials(table_ref, index_ref, quadrant_ref, poly_ref)
    load_variance.wait()

    live = count_ref[0]

    def invert(b, carry):
        flag = (b < live).astype(jnp.float32)
        rows = pl.ds(pl.multiple_of(b * STRIP, STRIP), STRIP)
        for chunk in range(BLOCK // STRIP):
            core, half, step = chunk // 8, chunk // 4 % 2, chunk % 4
            strips_ref[half * 8 + step * 2 + core, rows, :] = flag / variance_ref[b, chunk * STRIP : (chunk + 1) * STRIP, :]
        return carry

    lax.fori_loop(0, BLOCKS, invert, 0)
    for unit in range(4):
        slots_ref[unit] = slot_rows(patches_ref, quadrants_ref, live, unit, here)
    pl.semaphore_wait(barrier, len(all_partners))

    def remote(src, dst, send, recv, to):
        return pltpu.make_async_remote_copy(
            src_ref=src, dst_ref=dst, send_sem=send, recv_sem=recv, device_id=to["id"], device_id_type=MESH
        )

    def slots_copy(unit, o):
        to = here.at(c=o % 2, **{UNITS[unit][2]: o // 2})
        return remote(slots_ref.at[unit], got_slots_ref.at[unit * 8 + o], slots_send.at[unit, o], slots_recv.at[unit, o], to)

    def first_copy(unit, o, rows):
        axis = UNITS[unit][2]
        to = here.at(c=o % 2, **{axis: o // 2})
        source = strips_ref.at[unit * 8 + to[axis] * 2 + to["c"], rows, :]
        target = got_ref.at[unit * 8 + here.strip(axis), rows, :]
        if o == 0:
            return pltpu.make_async_copy(source, target, first_recv.at[unit, 0])
        return remote(source, target, first_send.at[unit, o], first_recv.at[unit, o], to)

    everything = pl.ds(0, SLAB)
    for unit in range(2):
        for o in range(8):
            first_copy(unit, o, everything).start()
    for unit in range(4):
        for o in range(1, 8):
            slots_copy(unit, o).start()
    load_image.wait()

    def compute(half, every, meanwhile):
        unit = 2 + half

        def step(group, carry):
            first = group * GROUP
            for core in range(2):

                def emit(b, total, core=core):
                    rows = pl.ds(pl.multiple_of(b * STRIP, STRIP), STRIP)
                    for step in range(SIDE):
                        at = step * 2 + core
                        strips_ref[unit * 8 + at, rows, :] = (
                            strips_ref[half * 8 + at, rows, :] * total[step * STRIP : (step + 1) * STRIP]
                        )

                matched_tile(core * 2 + half, first, image_ref, left_ref, right_ref, poly_ref, parts_ref, emit)

            def send():
                size = every * GROUP * STRIP
                rows = pl.ds(pl.multiple_of(lax.div(group, every) * size, size), size)
                for o in range(8):
                    first_copy(unit, o, rows).start()

            if every == 1:
                send()
            else:
                pl.when(lax.rem(group, every) == every - 1)(send)
            for after, run in meanwhile:
                pl.when(group == after)(run)
            return carry

        lax.fori_loop(0, BLOCKS // GROUP, step, 0)

    def take_slots(unit):
        for o in range(1, 8):
            slots_copy(unit, o).wait_recv()

    def choose(own, home, away):
        if own is True:
            home()
        elif own is False:
            away()
        else:
            pl.when(own)(home)
            pl.when(jnp.logical_not(own))(away)

    def nothing():
        pass

    def halved(unit, axis):
        return axis == "y" and UNITS[unit][2] != "y"

    def steps(unit, axis):
        if halved(unit, axis):
            for m in range(2):
                rise = here.odd + 2 * m
                to = here.at(y=rise)
                yield rise, to, lax.div(to["y"], 2), (here.odd == 0 if m == 0 else False)
        else:
            for o in range(SIDE):
                to = here.at(**{axis: o})
                yield o, to, to[axis], o == 0

    def width(unit):
        return 8 if UNITS[unit][2] == "y" else 16

    def line(unit, second):
        axis = UNITS[unit][3][second]
        slots = width(unit)
        if not second:
            slots = slots * (2 if halved(unit, UNITS[unit][3][1]) else SIDE)
        source, target = (middle_ref, far_ref) if second else (dense_ref, near_ref)
        for at, (o, to, share, own) in enumerate(steps(unit, axis)):
            part = source.at[unit, :, pl.ds(pl.multiple_of(share * slots, 8), slots), :]
            place = target.at[unit, o, :, pl.ds(0, slots), :]
            arrived = second_recv.at[unit, 4 * second + o]
            yield (
                pltpu.make_async_copy(part, place, arrived) if own is not False else None,
                remote(part, place, second_send.at[unit, 4 * second + at], arrived, to) if own is not True else None,
                own,
            )

    def plane(unit):
        slots = width(unit)
        first, last = (a for a in "xzy" if a != UNITS[unit][2])
        for at, ((o, to, share, own), (p, on, more, also)) in enumerate(
            itertools.product(steps(unit, first), steps(unit, last))
        ):
            to = dict(to, **{last: on[last]})
            to["id"] = (to["y"], (to["x"] * SIDE + to["z"]) * 2 + to["c"])
            base = pl.multiple_of((share * (2 if halved(unit, last) else SIDE) + more) * slots, 8)
            part = dense_ref.at[unit, :, pl.ds(base, slots), :]
            place = sums_ref.at[o * SIDE + p, :, pl.ds(0, slots), :]
            arrived = second_recv.at[unit, o * SIDE + p]
            own = False if own is False or also is False else also if own is True else own
            yield (
                pltpu.make_async_copy(part, place, arrived) if own is not False else None,
                remote(part, place, second_send.at[unit, at], arrived, to) if own is not True else None,
                own,
            )

    def start_all(copies):
        for home, away, own in copies:
            choose(own, home and home.start, away and away.start)

    def end_all(copies):
        for home, away, own in copies:
            choose(own, nothing, away and away.wait_send)

    def start_second(unit):
        start_all(plane(unit) if UNITS[unit][3] == "plane" else line(unit, 0))

    def arrived_sum(source, slots, unit, sems):
        for n, at in enumerate(sems):
            part = source.at[n, :, pl.ds(0, slots), :]
            pltpu.make_async_copy(part, part, second_recv.at[unit, at]).wait()

    def where_owner(unit, axis, run):
        if halved(unit, axis):
            pl.when(here.odd == 0)(run)
        else:
            run()

    def pass_on(unit):
        first, last = UNITS[unit][3]
        slots = width(unit) * (2 if halved(unit, last) else SIDE)

        def run():
            arrived_sum(near_ref.at[unit], slots, unit, range(4))
            for row in range(STRIP):
                total = near_ref[unit, 0, row, :slots, :]
                for o in range(1, SIDE):
                    total = total + near_ref[unit, o, row, :slots, :]
                middle_ref[unit, row, :slots, :] = total
            start_all(line(unit, 1))

        where_owner(unit, first, run)

    def end_second(unit):
        if UNITS[unit][3] == "plane":
            end_all(plane(unit))
        else:
            end_all(line(unit, 0))
            where_owner(unit, UNITS[unit][3][0], lambda: end_all(line(unit, 1)))

    def gather(unit):
        for o in range(8):
            if o == 0:
                first_copy(unit, 0, everything).wait()
            else:
                first_copy(unit, o, everything).wait_recv()
        take_slots(unit)
        slots = slots_ref[unit]
        for o in range(1, 8):
            slots = jnp.maximum(slots, got_slots_ref[unit * 8 + o])
        hot = lax.broadcasted_iota(jnp.int32, (SLOTS, 256), 0) == slots[0:1, :]
        hot = hot.astype(jnp.float32).astype(jnp.bfloat16)
        for row in range(STRIP):
            data = jnp.concatenate(
                [got_ref[unit * 8 + o, pl.ds(row, BLOCKS, stride=STRIP), :] for o in range(8)], axis=0
            )
            both = jnp.dot(hot, jnp.concatenate(split(data), axis=1), preferred_element_type=jnp.float32)
            dense_ref[unit, row] = both[:, :BLOCK] + both[:, BLOCK:]
        start_second(unit)

    def third_copies(unit):
        axis = UNITS[unit][2]
        if axis == "y":
            for o in range(4):
                down, c = o // 2, o % 2
                to = here.at(c=c)
                owner = here.c + 2 * down
                to["id"] = (owner, to["id"][1])
                yield o, to, to["c"] * 2 + down, (owner == here.y if c == 0 else False)
        else:
            for o in range(8):
                to = here.at(c=o % 2, **{axis: o // 2})
                yield o, to, to[axis] * 2 + to["c"], o == 0

    def third_refs(unit, o, to, at):
        axis = UNITS[unit][2]
        source = final_ref.at[unit, pl.ds(pl.multiple_of(at * 16, 16), 16), :]
        where = getattr(here, axis)
        target = got_final_ref.at[unit, where]
        away = remote(source, target, third_send.at[unit, o], third_recv.at[unit, where], to)
        return away, pltpu.make_async_copy(source, target, third_recv.at[unit, where])

    def reduce(unit):
        axis = UNITS[unit][2]
        slots = width(unit)

        def run():
            if UNITS[unit][3] == "plane":
                source, sems = sums_ref, range(16)
            else:
                source, sems = far_ref.at[unit], range(4, 8)
            arrived_sum(source, slots, unit, sems)
            for row in range(STRIP):
                total = source[0, row, :slots, :]
                for o in range(1, len(sems)):
                    total = total + source[o, row, :slots, :]
                final_ref[unit, pl.ds(row, slots, stride=STRIP), :] = total
            for o, to, at, own in third_copies(unit):
                away, home = third_refs(unit, o, to, at)
                if own is True:
                    home.start()
                elif own is False:
                    away.start()
                else:
                    pl.when(own)(home.start)
                    pl.when(jnp.logical_not(own))(away.start)

        if axis == "y":
            run()
        else:
            pl.when(here.odd == 0)(run)

    def end_third(unit):
        def run():
            for o, to, at, own in third_copies(unit):
                away, _ = third_refs(unit, o, to, at)
                if own is True:
                    continue
                if own is False:
                    away.wait_send()
                else:
                    pl.when(jnp.logical_not(own))(away.wait_send)

        if UNITS[unit][2] == "y":
            run()
        else:
            pl.when(here.odd == 0)(run)

    def finish(unit):
        array, half = UNITS[unit][:2]
        for step in range(SIDE):
            part = got_final_ref.at[unit, step]
            pltpu.make_async_copy(part, part, third_recv.at[unit, step]).wait()
            rows = slice(half * TILE + step * STRIP, half * TILE + (step + 1) * STRIP)
            out_ref[array, rows, :BLOCK] = got_final_ref[unit, step, :STRIP, :]
            out_ref[array, rows, BLOCK:] = got_final_ref[unit, step, STRIP:, :]

    def gather_inverses():
        gather(0)
        gather(1)

    compute(0, 2, ())
    compute(1, 1, ((1, gather_inverses), (2, lambda: gather(2))))
    for unit in range(3):
        pass_on(unit)
    gather(3)
    for unit in range(3):
        reduce(unit)
    for unit in range(3):
        finish(unit)
    reduce(3)
    finish(3)
    for unit in range(4):
        for o in range(1, 8):
            slots_copy(unit, o).wait_send()
        for o in range(1, 8):
            first_copy(unit, o, everything).wait_send()
        end_second(unit)
        end_third(unit)


def fused(count, quadrants, *arrays):
    vmem = pl.BlockSpec(memory_space=pltpu.VMEM)
    smem = pl.BlockSpec(memory_space=pltpu.SMEM)
    dma = pltpu.SemaphoreType.DMA
    f32, bf16 = jnp.float32, jnp.bfloat16
    units = len(UNITS)
    return pl.pallas_call(
        fused_kernel,
        out_shape=jax.ShapeDtypeStruct((2, 64, 256), f32),
        in_specs=[smem, smem] + [pl.BlockSpec(memory_space=pl.ANY)] * 2 + [vmem] * (len(arrays) - 2),
        out_specs=vmem,
        scratch_shapes=[
            pltpu.VMEM((BLOCKS, BLOCK, BLOCK), f32),
            pltpu.VMEM((BLOCKS, BLOCK, BLOCK), f32),
            dma((2,)),
            pltpu.VMEM((NB * TILE, 256), bf16),
            pltpu.VMEM((NB, 256, 256), bf16),
            pltpu.VMEM((BLOCKS, 3, NB, BLOCK), f32),
            pltpu.VMEM((NB, GROUP * TILE, 256), bf16),
            pltpu.VMEM((units * 8, SLAB, BLOCK), f32),
            pltpu.VMEM((units, 8, 256), jnp.int32),
            pltpu.VMEM((units * 8, 8, 256), jnp.int32),
            pltpu.VMEM((units * 8, SLAB, BLOCK), f32),
            pltpu.VMEM((units, STRIP, SLOTS, BLOCK), f32),
            pltpu.VMEM((units, SIDE, STRIP, 64, BLOCK), f32),
            pltpu.VMEM((units, STRIP, 64, BLOCK), f32),
            pltpu.VMEM((units, SIDE, STRIP, 16, BLOCK), f32),
            pltpu.VMEM((16, STRIP, 16, BLOCK), f32),
            pltpu.VMEM((units, 16 * STRIP, BLOCK), f32),
            pltpu.VMEM((units, SIDE, 2 * STRIP, BLOCK), f32),
            dma((units, 8)), dma((units, 8)),
            dma((units, 8)), dma((units, 8)),
            dma((units, 16)), dma((units, 16)),
            dma((units, 8)), dma((units, SIDE)),
        ],
        compiler_params=pltpu.CompilerParams(collective_id=0, has_side_effects=True, vmem_limit_bytes=56 << 20),
        name="coadd",
    )(count, quadrants, *arrays)


def on_device(
    image, variance, dest_patch, quadrant, coef_index, block_count, coef_table, row_taps, col_taps
):
    table = coef_table.transpose(2, 1, 0).reshape(-1, coef_table.shape[0])
    sums = fused(
        block_count[0], quadrant[0, 0], image[0, 0], variance[0, 0], row_taps, col_taps, table,
        coef_index[0], dest_patch[0], quadrant[0],
    )
    return sums[1][None], sums[0][None]


def solution(mesh):
    placed = (
        P("visit", "patch", None, None, None),
        P("visit", "patch", None, None, None),
        P("visit", "patch", None),
        P("visit", "patch", None),
        P("visit", "patch", None),
        P("visit", "patch"),
        P(),
        P(),
        P(),
    )
    return jax.shard_map(
        on_device,
        mesh=mesh,
        in_specs=placed,
        out_specs=(P("patch", "visit", None), P("patch", "visit", None)),
        check_vma=False,
    )
```

```python
import itertools

import jax
import jax.numpy as jnp
from jax import lax
from jax.experimental import pallas as pl
from jax.experimental.pallas import tpu as pltpu
from jax.sharding import PartitionSpec as P

BLOCK = 128
TAPS = 41
REACH = TAPS // 2
NB = 16
BLOCKS = 32
TILE = 32
WIN = 80
LEAD = 24
GROUP = 8
STRIP = 8
SIDE = 4
SLOTS = 128
SLAB = BLOCKS * STRIP
FULL = SLAB + STRIP
MESH = pl.DeviceIdType.MESH
UNITS = ((0, 0, "x", "zy"), (0, 1, "z", "yx"), (1, 0, "y", "zx"), (1, 1, "x", "plane"))
AXES = ("x", "y", "z")


def split(x):
    high = x.astype(jnp.bfloat16)
    return high, (x - high.astype(jnp.float32)).astype(jnp.bfloat16)


def build_bands(row_ref, col_ref, left_ref, right_ref):
    tap = lax.broadcasted_iota(jnp.int32, (TAPS, 256), 0)
    lane = lax.broadcasted_iota(jnp.int32, (TAPS, 256), 1)

    def place(parts, *found):
        hot = [f.astype(jnp.float32).astype(jnp.bfloat16) for f in found]
        return sum(jnp.dot(p, h, preferred_element_type=jnp.float32) for p, h in zip(parts, hot))

    at = LEAD + REACH - tap
    spread_rows = place(split(col_ref[...]), (lane == at) | (lane == at + 2 * WIN), lane == at + WIN)
    at = lax.rem(tap + (BLOCK - REACH), BLOCK)
    high, low = split(row_ref[...])
    row_high, row_low = place((high,), lane == at)[:, :BLOCK], place((low,), lane == at)[:, :BLOCK]
    near = lax.broadcasted_iota(jnp.int32, (BLOCK, BLOCK), 1) - lax.broadcasted_iota(jnp.int32, (BLOCK, BLOCK), 0)
    near = (near <= REACH) & (near >= -REACH)

    def roll(row, height):
        return pltpu.roll(jnp.broadcast_to(row, (height, row.shape[1])), 0, 1, stride=1, stride_axis=0)

    for k in range(NB):
        band = roll(spread_rows[k : k + 1, :], TILE)
        left_ref[k * TILE : (k + 1) * TILE, :] = band.astype(jnp.bfloat16)
        high = jnp.where(near, roll(row_high[k : k + 1, :], BLOCK), 0.0).astype(jnp.bfloat16)
        low = jnp.where(near, roll(row_low[k : k + 1, :], BLOCK), 0.0).astype(jnp.bfloat16)
        right_ref[k, :BLOCK, :BLOCK] = high
        right_ref[k, :BLOCK, BLOCK:] = low
        right_ref[k, BLOCK:, :BLOCK] = high
        right_ref[k, BLOCK:, BLOCK:] = jnp.zeros_like(low)


def build_polynomials(table_ref, index_ref, quadrant_ref, poly_ref):
    entry = lax.broadcasted_iota(jnp.int32, (table_ref.shape[1], BLOCK), 0)
    index = jnp.concatenate([index_ref[...]] * (BLOCK // BLOCKS), axis=1)
    hot = (entry == index).astype(jnp.float32).astype(jnp.bfloat16)
    rest, coefs = table_ref[...], None
    for _ in range(3):
        part = rest.astype(jnp.bfloat16)
        rest = rest - part.astype(jnp.float32)
        picked = jnp.dot(part, hot, preferred_element_type=jnp.float32)
        coefs = picked if coefs is None else coefs + picked
    column = lax.broadcasted_iota(jnp.int32, (NB, BLOCK), 1).astype(jnp.float32)
    own = (column + 0.5) / BLOCK - 1.0
    for b in range(BLOCKS):
        quadrant = quadrant_ref[b]
        down = (quadrant // 2).astype(jnp.float32)
        u = own + (quadrant % 2).astype(jnp.float32)
        a = [jnp.broadcast_to(coefs[m * NB : (m + 1) * NB, b : b + 1], (NB, BLOCK)) for m in range(6)]
        q = a[0] + u * (a[1] + u * a[3])
        s = a[2] + u * a[4]
        e = a[5]
        poly_ref[b, 0] = q + down * (s + down * e)
        poly_ref[b, 1] = s + (2.0 * down) * e
        poly_ref[b, 2] = e


def window(image_ref, block, tile):
    start = TILE * tile - LEAD
    low, high = max(start, 0), min(start + WIN, BLOCK)
    part = image_ref[block, low:high, :]
    pieces = []
    if low > start:
        pieces.append(jnp.zeros((low - start, BLOCK), jnp.float32))
    pieces.append(part)
    if high < start + WIN:
        pieces.append(jnp.zeros((start + WIN - high, BLOCK), jnp.float32))
    return jnp.concatenate(pieces, axis=0) if len(pieces) > 1 else part


def matched_tile(tile, first, image_ref, left_ref, right_ref, poly_ref, parts_ref, emit):
    for pair in range(GROUP // 2):
        both = jnp.concatenate(
            [window(image_ref, first + 2 * pair, tile), window(image_ref, first + 2 * pair + 1, tile)], axis=1
        )
        high, low = split(both)
        rhs = jnp.concatenate([high, high, low, jnp.zeros((256 - 3 * WIN, 2 * BLOCK), jnp.bfloat16)], axis=0)
        spread = jnp.dot(left_ref[...], rhs, preferred_element_type=jnp.float32)
        for side in range(2):
            high, low = split(spread[:, side * BLOCK : (side + 1) * BLOCK])
            at = (2 * pair + side) * TILE
            parts_ref[:, at : at + TILE, :BLOCK] = high.reshape(NB, TILE, BLOCK)
            parts_ref[:, at : at + TILE, BLOCK:] = low.reshape(NB, TILE, BLOCK)
    t = (lax.broadcasted_iota(jnp.int32, (TILE, BLOCK), 0).astype(jnp.float32) + (TILE * tile + 0.5)) / BLOCK - 1.0
    total = [None] * GROUP
    for k in range(NB):
        both = jnp.dot(parts_ref[k], right_ref[k], preferred_element_type=jnp.float32)
        basis = both[:, :BLOCK] + both[:, BLOCK:]
        for block in range(GROUP):
            q = poly_ref[first + block, 0, k : k + 1, :]
            s = poly_ref[first + block, 1, k : k + 1, :]
            e = poly_ref[first + block, 2, k : k + 1, :]
            term = (q + t * (s + t * e)) * basis[block * TILE : (block + 1) * TILE]
            total[block] = term if total[block] is None else total[block] + term
    for block in range(GROUP):
        emit(first + block, total[block])


class Here:
    def __init__(self):
        self.y = lax.axis_index("visit")
        place = lax.axis_index("patch")
        self.x, self.z, self.c = lax.div(place, 8), lax.rem(lax.div(place, 2), 4), lax.rem(place, 2)
        self.odd = lax.rem(self.y + self.c, 2)

    def strip(self, axis):
        return getattr(self, axis) * 2 + self.c

    def at(self, c=0, **offsets):
        place = {axis: lax.rem(getattr(self, axis) + offsets.get(axis, 0), SIDE) for axis in AXES}
        place["c"] = lax.rem(self.c + c, 2)
        place["id"] = (place["y"], (place["x"] * SIDE + place["z"]) * 2 + place["c"])
        return place


def partners():
    found = set()
    for _, _, axis, later in UNITS:
        for step, c in itertools.product(range(SIDE), range(2)):
            found.add(tuple(step if a == axis else 0 for a in AXES) + (c,))
        others = [a for a in AXES if a != axis]
        for steps in itertools.product(range(SIDE), repeat=2):
            if later == "plane" or 0 in steps:
                to = dict(zip(others, steps))
                found.add(tuple(to.get(a, 0) for a in AXES) + (0,))
    found.discard((0, 0, 0, 0))
    return sorted(found)


def slot_rows(patches, quadrants, live, unit, here):
    _, _, axis, later = UNITS[unit]
    patch, quadrant = (jnp.concatenate([ref[...]] * 8, axis=1) for ref in (patches, quadrants))
    part = {"x": lax.div(patch, 8), "z": lax.rem(lax.div(patch, 2), 4)}
    sizes = {"x": 4, "z": 4, "y": 2}
    c = lax.rem(patch, 2)
    down, across = lax.div(quadrant, 2), lax.rem(quadrant, 2)
    part["y"] = down
    order = later if later != "plane" else "".join(a for a in "xzy" if a != axis)
    slot = part[order[0]] * sizes[order[1]] + part[order[1]]
    if axis == "y":
        slot = slot * 8 + c * 4 + down * 2 + across
    else:
        slot = slot * 16 + part[axis] * 4 + c * 2 + across
    lane = lax.broadcasted_iota(jnp.int32, slot.shape, 1)
    at = lane - here.strip(axis) * BLOCKS
    mine = (at >= 0) & (at < jnp.minimum(live, BLOCKS))
    slot = jnp.broadcast_to(jnp.where(mine, slot, -1).astype(jnp.float32), (STRIP, 256))
    row = lax.broadcasted_iota(jnp.int32, (STRIP, BLOCK), 0)
    return jnp.where(row == 0, slot[:, :BLOCK], slot[:, BLOCK:])


def fused_kernel(
    count_ref, quadrant_ref, image_hbm, variance_hbm, row_ref, col_ref, table_ref, index_ref, patches_ref, quadrants_ref,
    out_ref,
    image_ref, variance_ref, load_sem, left_ref, right_ref, poly_ref, parts_ref, strips_ref, got_ref, dense_ref, near_ref, middle_ref, far_ref, sums_ref,
    final_ref, got_final_ref,
    first_send, first_recv, second_send, second_recv, third_send, third_recv,
):
    here = Here()
    barrier = pltpu.get_barrier_semaphore()
    all_partners = partners()
    for x, y, z, c in all_partners:
        pl.semaphore_signal(barrier, inc=1, device_id=here.at(x=x, y=y, z=z, c=c)["id"], device_id_type=MESH)

    load_variance = pltpu.make_async_copy(variance_hbm, variance_ref, load_sem.at[0])
    load_image = pltpu.make_async_copy(image_hbm, image_ref, load_sem.at[1])
    load_variance.start()
    load_image.start()
    live = count_ref[0]
    for unit in range(3):
        ids = slot_rows(patches_ref, quadrants_ref, live, unit, here)
        for at in range(8):
            strips_ref[unit * 8 + at, SLAB:, :] = ids

    def invert(half):
        def step(b, carry):
            flag = (b < live).astype(jnp.float32)
            rows = pl.ds(pl.multiple_of(b * STRIP, STRIP), STRIP)
            for core, step in itertools.product(range(2), range(SIDE)):
                first = core * 64 + half * TILE + step * STRIP
                strips_ref[half * 8 + step * 2 + core, rows, :] = flag / variance_ref[b, first : first + STRIP, :]
            return carry

        lax.fori_loop(0, BLOCKS, step, 0)

    def remote(src, dst, send, recv, to):
        return pltpu.make_async_remote_copy(
            src_ref=src, dst_ref=dst, send_sem=send, recv_sem=recv, device_id=to["id"], device_id_type=MESH
        )

    def first_copy(unit, o, rows):
        axis = UNITS[unit][2]
        to = here.at(c=o % 2, **{axis: o // 2})
        source = strips_ref.at[unit * 8 + to[axis] * 2 + to["c"], rows, :]
        target = got_ref.at[unit * 8 + here.strip(axis), rows, :]
        if o == 0:
            return pltpu.make_async_copy(source, target, first_recv.at[unit, 0])
        return remote(source, target, first_send.at[unit, o], first_recv.at[unit, o], to)

    def all_rows(unit):
        return pl.ds(0, SLAB if unit == 3 else FULL)

    load_variance.wait()
    invert(0)
    pl.semaphore_wait(barrier, len(all_partners))
    for o in range(8):
        first_copy(0, o, all_rows(0)).start()
    invert(1)
    for o in range(8):
        first_copy(1, o, all_rows(1)).start()
    build_bands(row_ref, col_ref, left_ref, right_ref)
    build_polynomials(table_ref, index_ref, quadrant_ref, poly_ref)
    load_image.wait()

    def compute(half, chunks, meanwhile):
        unit = 2 + half

        def step(group, carry):
            first = group * GROUP
            for core in range(2):

                def emit(b, total, core=core):
                    rows = pl.ds(pl.multiple_of(b * STRIP, STRIP), STRIP)
                    for step in range(SIDE):
                        at = step * 2 + core
                        strips_ref[unit * 8 + at, rows, :] = (
                            strips_ref[half * 8 + at, rows, :] * total[step * STRIP : (step + 1) * STRIP]
                        )

                matched_tile(core * 2 + half, first, image_ref, left_ref, right_ref, poly_ref, parts_ref, emit)

            for after, begin, end in chunks:

                @pl.when(group == after)
                def send(begin=begin, end=end):
                    for o in range(8):
                        first_copy(unit, o, pl.ds(begin, end - begin)).start()

            for after, run in meanwhile:
                pl.when(group == after)(run)
            return carry

        lax.fori_loop(0, BLOCKS // GROUP, step, 0)

    def choose(own, home, away):
        if own is True:
            home()
        elif own is False:
            away()
        else:
            pl.when(own)(home)
            pl.when(jnp.logical_not(own))(away)

    def nothing():
        pass

    def halved(unit, axis):
        return axis == "y" and UNITS[unit][2] != "y"

    def steps(unit, axis):
        if halved(unit, axis):
            for m in range(2):
                rise = here.odd + 2 * m
                to = here.at(y=rise)
                yield rise, to, lax.div(to["y"], 2), (here.odd == 0 if m == 0 else False)
        else:
            for o in range(SIDE):
                to = here.at(**{axis: o})
                yield o, to, to[axis], o == 0

    def width(unit):
        return 8 if UNITS[unit][2] == "y" else 16

    def line(unit, second):
        axis = UNITS[unit][3][second]
        slots = width(unit)
        if not second:
            slots = slots * (2 if halved(unit, UNITS[unit][3][1]) else SIDE)
        source, target = (middle_ref, far_ref) if second else (dense_ref, near_ref)
        for at, (o, to, share, own) in enumerate(steps(unit, axis)):
            part = source.at[unit, :, pl.ds(pl.multiple_of(share * slots, 8), slots), :]
            place = target.at[unit, o, :, pl.ds(0, slots), :]
            arrived = second_recv.at[unit, 4 * second + o]
            yield (
                pltpu.make_async_copy(part, place, arrived) if own is not False else None,
                remote(part, place, second_send.at[unit, 4 * second + at], arrived, to) if own is not True else None,
                own,
            )

    def plane(unit):
        slots = width(unit)
        first, last = (a for a in "xzy" if a != UNITS[unit][2])
        for at, ((o, to, share, own), (p, on, more, also)) in enumerate(
            itertools.product(steps(unit, first), steps(unit, last))
        ):
            to = dict(to, **{last: on[last]})
            to["id"] = (to["y"], (to["x"] * SIDE + to["z"]) * 2 + to["c"])
            base = pl.multiple_of((share * (2 if halved(unit, last) else SIDE) + more) * slots, 8)
            part = dense_ref.at[unit, :, pl.ds(base, slots), :]
            place = sums_ref.at[o * SIDE + p, :, pl.ds(0, slots), :]
            arrived = second_recv.at[unit, o * SIDE + p]
            own = False if own is False or also is False else also if own is True else own
            yield (
                pltpu.make_async_copy(part, place, arrived) if own is not False else None,
                remote(part, place, second_send.at[unit, at], arrived, to) if own is not True else None,
                own,
            )

    def start_all(copies):
        for home, away, own in copies:
            choose(own, home and home.start, away and away.start)

    def end_all(copies):
        for home, away, own in copies:
            choose(own, nothing, away and away.wait_send)

    def start_second(unit):
        start_all(plane(unit) if UNITS[unit][3] == "plane" else line(unit, 0))

    def arrived_sum(source, slots, unit, sems):
        for n, at in enumerate(sems):
            part = source.at[n, :, pl.ds(0, slots), :]
            pltpu.make_async_copy(part, part, second_recv.at[unit, at]).wait()

    def where_owner(unit, axis, run):
        if halved(unit, axis):
            pl.when(here.odd == 0)(run)
        else:
            run()

    def pass_on(unit):
        first, last = UNITS[unit][3]
        slots = width(unit) * (2 if halved(unit, last) else SIDE)

        def run():
            arrived_sum(near_ref.at[unit], slots, unit, range(4))
            for row in range(STRIP):
                total = near_ref[unit, 0, row, :slots, :]
                for o in range(1, SIDE):
                    total = total + near_ref[unit, o, row, :slots, :]
                middle_ref[unit, row, :slots, :] = total
            start_all(line(unit, 1))

        where_owner(unit, first, run)

    def end_second(unit):
        if UNITS[unit][3] == "plane":
            end_all(plane(unit))
        else:
            end_all(line(unit, 0))
            where_owner(unit, UNITS[unit][3][0], lambda: end_all(line(unit, 1)))

    def gather(unit):
        for o in range(8):
            if o == 0:
                first_copy(unit, 0, all_rows(unit)).wait()
            else:
                first_copy(unit, o, all_rows(unit)).wait_recv()
        ids = got_ref[unit % 3 * 8, SLAB:, :]
        for o in range(1, 8):
            ids = jnp.maximum(ids, got_ref[unit % 3 * 8 + o, SLAB:, :])
        ids = jnp.concatenate([ids[0:1, :], ids[1:2, :]], axis=1)
        hot = lax.broadcasted_iota(jnp.int32, (SLOTS, 256), 0).astype(jnp.float32) == ids
        hot = hot.astype(jnp.float32).astype(jnp.bfloat16)
        for row in range(STRIP):
            data = jnp.concatenate(
                [got_ref[unit * 8 + o, pl.ds(row, BLOCKS, stride=STRIP), :] for o in range(8)], axis=0
            )
            both = jnp.dot(hot, jnp.concatenate(split(data), axis=1), preferred_element_type=jnp.float32)
            dense_ref[unit, row] = both[:, :BLOCK] + both[:, BLOCK:]
        start_second(unit)

    def third_copies(unit):
        axis = UNITS[unit][2]
        if axis == "y":
            for o in range(4):
                down, c = o // 2, o % 2
                to = here.at(c=c)
                owner = here.c + 2 * down
                to["id"] = (owner, to["id"][1])
                yield o, to, to["c"] * 2 + down, (owner == here.y if c == 0 else False)
        else:
            for o in range(8):
                to = here.at(c=o % 2, **{axis: o // 2})
                yield o, to, to[axis] * 2 + to["c"], o == 0

    def third_refs(unit, o, to, at):
        axis = UNITS[unit][2]
        source = final_ref.at[unit, pl.ds(pl.multiple_of(at * 16, 16), 16), :]
        where = getattr(here, axis)
        target = got_final_ref.at[unit, where]
        away = remote(source, target, third_send.at[unit, o], third_recv.at[unit, where], to)
        return away, pltpu.make_async_copy(source, target, third_recv.at[unit, where])

    def reduce(unit):
        axis = UNITS[unit][2]
        slots = width(unit)

        def run():
            if UNITS[unit][3] == "plane":
                source, sems = sums_ref, range(16)
            else:
                source, sems = far_ref.at[unit], range(4, 8)
            arrived_sum(source, slots, unit, sems)
            for row in range(STRIP):
                total = source[0, row, :slots, :]
                for o in range(1, len(sems)):
                    total = total + source[o, row, :slots, :]
                final_ref[unit, pl.ds(row, slots, stride=STRIP), :] = total
            for o, to, at, own in third_copies(unit):
                away, home = third_refs(unit, o, to, at)
                if own is True:
                    home.start()
                elif own is False:
                    away.start()
                else:
                    pl.when(own)(home.start)
                    pl.when(jnp.logical_not(own))(away.start)

        if axis == "y":
            run()
        else:
            pl.when(here.odd == 0)(run)

    def end_third(unit):
        def run():
            for o, to, at, own in third_copies(unit):
                away, _ = third_refs(unit, o, to, at)
                if own is True:
                    continue
                if own is False:
                    away.wait_send()
                else:
                    pl.when(jnp.logical_not(own))(away.wait_send)

        if UNITS[unit][2] == "y":
            run()
        else:
            pl.when(here.odd == 0)(run)

    def finish(unit):
        array, half = UNITS[unit][:2]
        for step in range(SIDE):
            part = got_final_ref.at[unit, step]
            pltpu.make_async_copy(part, part, third_recv.at[unit, step]).wait()
            rows = slice(half * TILE + step * STRIP, half * TILE + (step + 1) * STRIP)
            out_ref[array, rows, :BLOCK] = got_final_ref[unit, step, :STRIP, :]
            out_ref[array, rows, BLOCK:] = got_final_ref[unit, step, STRIP:, :]

    def gather_inverses():
        gather(0)
        gather(1)

    compute(0, ((1, 0, SLAB // 2), (3, SLAB // 2, FULL)), ())
    compute(1, [(g, g * SLAB // 4, (g + 1) * SLAB // 4) for g in range(4)], ((1, gather_inverses), (2, lambda: gather(2))))
    for unit in range(3):
        pass_on(unit)
    gather(3)
    for unit in range(3):
        reduce(unit)
    for unit in range(3):
        finish(unit)
    reduce(3)
    finish(3)
    for unit in range(4):
        for o in range(1, 8):
            first_copy(unit, o, all_rows(unit)).wait_send()
        end_second(unit)
        end_third(unit)


def fused(count, quadrants, *arrays):
    vmem = pl.BlockSpec(memory_space=pltpu.VMEM)
    smem = pl.BlockSpec(memory_space=pltpu.SMEM)
    dma = pltpu.SemaphoreType.DMA
    f32, bf16 = jnp.float32, jnp.bfloat16
    units = len(UNITS)
    return pl.pallas_call(
        fused_kernel,
        out_shape=jax.ShapeDtypeStruct((2, 64, 256), f32),
        in_specs=[smem, smem] + [pl.BlockSpec(memory_space=pl.ANY)] * 2 + [vmem] * (len(arrays) - 2),
        out_specs=vmem,
        scratch_shapes=[
            pltpu.VMEM((BLOCKS, BLOCK, BLOCK), f32),
            pltpu.VMEM((BLOCKS, BLOCK, BLOCK), f32),
            dma((2,)),
            pltpu.VMEM((NB * TILE, 256), bf16),
            pltpu.VMEM((NB, 256, 256), bf16),
            pltpu.VMEM((BLOCKS, 3, NB, BLOCK), f32),
            pltpu.VMEM((NB, GROUP * TILE, 256), bf16),
            pltpu.VMEM((units * 8, FULL, BLOCK), f32),
            pltpu.VMEM((units * 8, FULL, BLOCK), f32),
            pltpu.VMEM((units, STRIP, SLOTS, BLOCK), f32),
            pltpu.VMEM((units, SIDE, STRIP, 64, BLOCK), f32),
            pltpu.VMEM((units, STRIP, 64, BLOCK), f32),
            pltpu.VMEM((units, SIDE, STRIP, 16, BLOCK), f32),
            pltpu.VMEM((16, STRIP, 16, BLOCK), f32),
            pltpu.VMEM((units, 16 * STRIP, BLOCK), f32),
            pltpu.VMEM((units, SIDE, 2 * STRIP, BLOCK), f32),
            dma((units, 8)), dma((units, 8)),
            dma((units, 16)), dma((units, 16)),
            dma((units, 8)), dma((units, SIDE)),
        ],
        compiler_params=pltpu.CompilerParams(collective_id=0, has_side_effects=True, vmem_limit_bytes=56 << 20),
        name="coadd",
    )(count, quadrants, *arrays)


def on_device(
    image, variance, dest_patch, quadrant, coef_index, block_count, coef_table, row_taps, col_taps
):
    table = coef_table.transpose(2, 1, 0).reshape(-1, coef_table.shape[0])
    sums = fused(
        block_count[0], quadrant[0, 0], image[0, 0], variance[0, 0], row_taps, col_taps, table,
        coef_index[0], dest_patch[0], quadrant[0],
    )
    return sums[1][None], sums[0][None]


def solution(mesh):
    placed = (
        P("visit", "patch", None, None, None),
        P("visit", "patch", None, None, None),
        P("visit", "patch", None),
        P("visit", "patch", None),
        P("visit", "patch", None),
        P("visit", "patch"),
        P(),
        P(),
        P(),
    )
    return jax.shard_map(
        on_device,
        mesh=mesh,
        in_specs=placed,
        out_specs=(P("patch", "visit", None), P("patch", "visit", None)),
        check_vma=False,
    )
```

```python
import itertools

import jax
import jax.numpy as jnp
from jax import lax
from jax.experimental import pallas as pl
from jax.experimental.pallas import tpu as pltpu
from jax.sharding import PartitionSpec as P

BLOCK = 128
TAPS = 41
REACH = TAPS // 2
NB = 16
BLOCKS = 32
TILE = 32
WIN = 80
LEAD = 24
GROUP = 8
STRIP = 8
SIDE = 4
SLOTS = 128
SLAB = BLOCKS * STRIP
FULL = SLAB + STRIP
MESH = pl.DeviceIdType.MESH
UNITS = ((0, 0, "y", "xz"), (0, 1, "x", "zy"), (1, 0, "z", "xy"), (1, 1, "y", "plane"))
AXES = ("x", "y", "z")


def split(x):
    high = x.astype(jnp.bfloat16)
    return high, (x - high.astype(jnp.float32)).astype(jnp.bfloat16)


def build_bands(row_ref, col_ref, left_ref, right_ref):
    tap = lax.broadcasted_iota(jnp.int32, (TAPS, 256), 0)
    lane = lax.broadcasted_iota(jnp.int32, (TAPS, 256), 1)

    def place(parts, *found):
        hot = [f.astype(jnp.float32).astype(jnp.bfloat16) for f in found]
        return sum(jnp.dot(p, h, preferred_element_type=jnp.float32) for p, h in zip(parts, hot))

    at = LEAD + REACH - tap
    spread_rows = place(split(col_ref[...]), (lane == at) | (lane == at + 2 * WIN), lane == at + WIN)
    at = lax.rem(tap + (BLOCK - REACH), BLOCK)
    high, low = split(row_ref[...])
    row_high, row_low = place((high,), lane == at)[:, :BLOCK], place((low,), lane == at)[:, :BLOCK]
    near = lax.broadcasted_iota(jnp.int32, (BLOCK, BLOCK), 1) - lax.broadcasted_iota(jnp.int32, (BLOCK, BLOCK), 0)
    near = (near <= REACH) & (near >= -REACH)

    def roll(row, height):
        return pltpu.roll(jnp.broadcast_to(row, (height, row.shape[1])), 0, 1, stride=1, stride_axis=0)

    for k in range(NB):
        band = roll(spread_rows[k : k + 1, :], TILE)
        left_ref[k * TILE : (k + 1) * TILE, :] = band.astype(jnp.bfloat16)
        high = jnp.where(near, roll(row_high[k : k + 1, :], BLOCK), 0.0).astype(jnp.bfloat16)
        low = jnp.where(near, roll(row_low[k : k + 1, :], BLOCK), 0.0).astype(jnp.bfloat16)
        right_ref[k, :BLOCK, :BLOCK] = high
        right_ref[k, :BLOCK, BLOCK:] = low
        right_ref[k, BLOCK:, :BLOCK] = high
        right_ref[k, BLOCK:, BLOCK:] = jnp.zeros_like(low)


def build_polynomials(table_ref, index_ref, quadrant_ref, poly_ref):
    entry = lax.broadcasted_iota(jnp.int32, (table_ref.shape[1], BLOCK), 0)
    index = jnp.concatenate([index_ref[...]] * (BLOCK // BLOCKS), axis=1)
    hot = (entry == index).astype(jnp.float32).astype(jnp.bfloat16)
    rest, coefs = table_ref[...], None
    for _ in range(3):
        part = rest.astype(jnp.bfloat16)
        rest = rest - part.astype(jnp.float32)
        picked = jnp.dot(part, hot, preferred_element_type=jnp.float32)
        coefs = picked if coefs is None else coefs + picked
    column = lax.broadcasted_iota(jnp.int32, (NB, BLOCK), 1).astype(jnp.float32)
    own = (column + 0.5) / BLOCK - 1.0
    for b in range(BLOCKS):
        quadrant = quadrant_ref[b]
        down = (quadrant // 2).astype(jnp.float32)
        u = own + (quadrant % 2).astype(jnp.float32)
        a = [jnp.broadcast_to(coefs[m * NB : (m + 1) * NB, b : b + 1], (NB, BLOCK)) for m in range(6)]
        q = a[0] + u * (a[1] + u * a[3])
        s = a[2] + u * a[4]
        e = a[5]
        poly_ref[b, 0] = q + down * (s + down * e)
        poly_ref[b, 1] = s + (2.0 * down) * e
        poly_ref[b, 2] = e


def window(image_ref, block, tile):
    start = TILE * tile - LEAD
    low, high = max(start, 0), min(start + WIN, BLOCK)
    part = image_ref[block, low:high, :]
    pieces = []
    if low > start:
        pieces.append(jnp.zeros((low - start, BLOCK), jnp.float32))
    pieces.append(part)
    if high < start + WIN:
        pieces.append(jnp.zeros((start + WIN - high, BLOCK), jnp.float32))
    return jnp.concatenate(pieces, axis=0) if len(pieces) > 1 else part


def matched_tile(tile, first, image_ref, left_ref, right_ref, poly_ref, parts_ref, emit):
    for pair in range(GROUP // 2):
        both = jnp.concatenate(
            [window(image_ref, first + 2 * pair, tile), window(image_ref, first + 2 * pair + 1, tile)], axis=1
        )
        high, low = split(both)
        rhs = jnp.concatenate([high, high, low, jnp.zeros((256 - 3 * WIN, 2 * BLOCK), jnp.bfloat16)], axis=0)
        spread = jnp.dot(left_ref[...], rhs, preferred_element_type=jnp.float32)
        for side in range(2):
            high, low = split(spread[:, side * BLOCK : (side + 1) * BLOCK])
            at = (2 * pair + side) * TILE
            parts_ref[:, at : at + TILE, :BLOCK] = high.reshape(NB, TILE, BLOCK)
            parts_ref[:, at : at + TILE, BLOCK:] = low.reshape(NB, TILE, BLOCK)
    t = (lax.broadcasted_iota(jnp.int32, (TILE, BLOCK), 0).astype(jnp.float32) + (TILE * tile + 0.5)) / BLOCK - 1.0
    total = [None] * GROUP
    for k in range(NB):
        both = jnp.dot(parts_ref[k], right_ref[k], preferred_element_type=jnp.float32)
        basis = both[:, :BLOCK] + both[:, BLOCK:]
        for block in range(GROUP):
            q = poly_ref[first + block, 0, k : k + 1, :]
            s = poly_ref[first + block, 1, k : k + 1, :]
            e = poly_ref[first + block, 2, k : k + 1, :]
            term = (q + t * (s + t * e)) * basis[block * TILE : (block + 1) * TILE]
            total[block] = term if total[block] is None else total[block] + term
    for block in range(GROUP):
        emit(first + block, total[block])


class Here:
    def __init__(self):
        self.y = lax.axis_index("visit")
        place = lax.axis_index("patch")
        self.x, self.z, self.c = lax.div(place, 8), lax.rem(lax.div(place, 2), 4), lax.rem(place, 2)
        self.odd = lax.rem(self.y + self.c, 2)
        self.seen = {}

    def strip(self, axis):
        return getattr(self, axis) * 2 + self.c

    def at(self, c=0, **offsets):
        key = (c,) + tuple(offsets.get(axis, 0) for axis in AXES)
        known = all(isinstance(step, int) for step in key)
        if known and key in self.seen:
            return dict(self.seen[key])
        place = {
            axis: lax.rem(getattr(self, axis) + step, SIDE) if not isinstance(step, int) or step else getattr(self, axis)
            for axis, step in zip(AXES, key[1:])
        }
        place["c"] = lax.rem(self.c + c, 2) if c else self.c
        place["id"] = (place["y"], (place["x"] * SIDE + place["z"]) * 2 + place["c"])
        if known:
            self.seen[key] = place
        return dict(place)


def partners():
    found = set()
    for _, _, axis, later in UNITS:
        for step, c in itertools.product(range(SIDE), range(2)):
            found.add(tuple(step if a == axis else 0 for a in AXES) + (c,))
        others = [a for a in AXES if a != axis]
        for steps in itertools.product(range(SIDE), repeat=2):
            if later == "plane" or 0 in steps:
                to = dict(zip(others, steps))
                found.add(tuple(to.get(a, 0) for a in AXES) + (0,))
    found.discard((0, 0, 0, 0))
    return sorted(found)


def slot_rows(patches, quadrants, live, unit, here):
    _, _, axis, later = UNITS[unit]
    patch, quadrant = (jnp.concatenate([ref[...]] * 8, axis=1) for ref in (patches, quadrants))
    part = {"x": lax.div(patch, 8), "z": lax.rem(lax.div(patch, 2), 4)}
    sizes = {"x": 4, "z": 4, "y": 2}
    c = lax.rem(patch, 2)
    down, across = lax.div(quadrant, 2), lax.rem(quadrant, 2)
    part["y"] = down
    order = later if later != "plane" else "".join(a for a in "xzy" if a != axis)
    slot = part[order[0]] * sizes[order[1]] + part[order[1]]
    if axis == "y":
        slot = slot * 8 + c * 4 + down * 2 + across
    else:
        slot = slot * 16 + part[axis] * 4 + c * 2 + across
    lane = lax.broadcasted_iota(jnp.int32, slot.shape, 1)
    at = lane - here.strip(axis) * BLOCKS
    mine = (at >= 0) & (at < jnp.minimum(live, BLOCKS))
    slot = jnp.broadcast_to(jnp.where(mine, slot, -1).astype(jnp.float32), (STRIP, 256))
    row = lax.broadcasted_iota(jnp.int32, (STRIP, BLOCK), 0)
    return jnp.where(row == 0, slot[:, :BLOCK], slot[:, BLOCK:])


def fused_kernel(
    count_ref, quadrant_ref, image_hbm, variance_hbm, row_ref, col_ref, table_ref, index_ref, patches_ref, quadrants_ref,
    out_ref,
    image_ref, variance_ref, load_sem, left_ref, right_ref, poly_ref, parts_ref, strips_ref, got_ref, dense_ref, near_ref, middle_ref, far_ref, sums_ref,
    final_ref, got_final_ref,
    first_send, first_recv, second_send, second_recv, third_send, third_recv,
):
    here = Here()
    barrier = pltpu.get_barrier_semaphore()
    all_partners = partners()
    here.at()
    for x, y, z, c in all_partners:
        pl.semaphore_signal(barrier, inc=1, device_id=here.at(x=x, y=y, z=z, c=c)["id"], device_id_type=MESH)

    load_variance = pltpu.make_async_copy(variance_hbm, variance_ref, load_sem.at[0])
    load_image = pltpu.make_async_copy(image_hbm, image_ref, load_sem.at[1])
    load_variance.start()
    load_image.start()
    live = count_ref[0]
    for unit in range(4):
        ids = slot_rows(patches_ref, quadrants_ref, live, unit, here)
        for at in range(8):
            strips_ref[unit * 8 + at, SLAB:, :] = ids

    def invert(half):
        def step(b, carry):
            flag = (b < live).astype(jnp.float32)
            rows = pl.ds(pl.multiple_of(b * STRIP, STRIP), STRIP)
            for core, step in itertools.product(range(2), range(SIDE)):
                first = core * 64 + half * TILE + step * STRIP
                strips_ref[half * 8 + step * 2 + core, rows, :] = flag / variance_ref[b, first : first + STRIP, :]
            return carry

        lax.fori_loop(0, BLOCKS, step, 0)

    def remote(src, dst, send, recv, to):
        return pltpu.make_async_remote_copy(
            src_ref=src, dst_ref=dst, send_sem=send, recv_sem=recv, device_id=to["id"], device_id_type=MESH
        )

    def first_copy(unit, o, rows):
        axis = UNITS[unit][2]
        to = here.at(c=o % 2, **{axis: o // 2})
        source = strips_ref.at[unit * 8 + to[axis] * 2 + to["c"], rows, :]
        target = got_ref.at[unit * 8 + here.strip(axis), rows, :]
        if o == 0:
            return pltpu.make_async_copy(source, target, first_recv.at[unit, 0])
        return remote(source, target, first_send.at[unit, o], first_recv.at[unit, o], to)

    load_variance.wait()
    invert(0)
    pl.semaphore_wait(barrier, len(all_partners))
    for o in range(8):
        first_copy(0, o, pl.ds(0, FULL)).start()
    invert(1)
    for o in range(8):
        first_copy(1, o, pl.ds(0, FULL)).start()
    build_bands(row_ref, col_ref, left_ref, right_ref)
    build_polynomials(table_ref, index_ref, quadrant_ref, poly_ref)
    load_image.wait()

    def compute(half, chunks, meanwhile):
        unit = 2 + half

        def step(group, carry):
            first = group * GROUP
            for core in range(2):

                def emit(b, total, core=core):
                    rows = pl.ds(pl.multiple_of(b * STRIP, STRIP), STRIP)
                    for step in range(SIDE):
                        at = step * 2 + core
                        strips_ref[unit * 8 + at, rows, :] = (
                            strips_ref[half * 8 + at, rows, :] * total[step * STRIP : (step + 1) * STRIP]
                        )

                matched_tile(core * 2 + half, first, image_ref, left_ref, right_ref, poly_ref, parts_ref, emit)

            for after, begin, end in chunks:

                @pl.when(group == after)
                def send(begin=begin, end=end):
                    for o in range(8):
                        first_copy(unit, o, pl.ds(begin, end - begin)).start()

            for after, run in meanwhile:
                pl.when(group == after)(run)
            return carry

        lax.fori_loop(0, BLOCKS // GROUP, step, 0)

    def choose(own, home, away):
        if own is True:
            home()
        elif own is False:
            away()
        else:
            pl.when(own)(home)
            pl.when(jnp.logical_not(own))(away)

    def nothing():
        pass

    def halved(unit, axis):
        return axis == "y" and UNITS[unit][2] != "y"

    def steps(unit, axis):
        if halved(unit, axis):
            for m in range(2):
                rise = here.odd + 2 * m
                to = here.at(y=rise)
                yield rise, to, lax.div(to["y"], 2), (here.odd == 0 if m == 0 else False)
        else:
            for o in range(SIDE):
                to = here.at(**{axis: o})
                yield o, to, to[axis], o == 0

    def width(unit):
        return 8 if UNITS[unit][2] == "y" else 16

    def line(unit, second):
        axis = UNITS[unit][3][second]
        slots = width(unit)
        if not second:
            slots = slots * (2 if halved(unit, UNITS[unit][3][1]) else SIDE)
        source, target = (middle_ref, far_ref) if second else (dense_ref, near_ref)
        for at, (o, to, share, own) in enumerate(steps(unit, axis)):
            part = source.at[unit, :, pl.ds(pl.multiple_of(share * slots, 8), slots), :]
            place = target.at[unit, o, :, pl.ds(0, slots), :]
            arrived = second_recv.at[unit, 4 * second + o]
            yield (
                pltpu.make_async_copy(part, place, arrived) if own is not False else None,
                remote(part, place, second_send.at[unit, 4 * second + at], arrived, to) if own is not True else None,
                own,
            )

    def plane(unit):
        slots = width(unit)
        first, last = (a for a in "xzy" if a != UNITS[unit][2])
        for at, ((o, to, share, own), (p, on, more, also)) in enumerate(
            itertools.product(steps(unit, first), steps(unit, last))
        ):
            to = dict(to, **{last: on[last]})
            to["id"] = (to["y"], (to["x"] * SIDE + to["z"]) * 2 + to["c"])
            base = pl.multiple_of((share * (2 if halved(unit, last) else SIDE) + more) * slots, 8)
            part = dense_ref.at[unit, :, pl.ds(base, slots), :]
            place = sums_ref.at[o * SIDE + p, :, pl.ds(0, slots), :]
            arrived = second_recv.at[unit, o * SIDE + p]
            own = False if own is False or also is False else also if own is True else own
            yield (
                pltpu.make_async_copy(part, place, arrived) if own is not False else None,
                remote(part, place, second_send.at[unit, at], arrived, to) if own is not True else None,
                own,
            )

    def start_all(copies):
        for home, away, own in copies:
            choose(own, home and home.start, away and away.start)

    def end_all(copies):
        for home, away, own in copies:
            choose(own, nothing, away and away.wait_send)

    def start_second(unit):
        start_all(plane(unit) if UNITS[unit][3] == "plane" else line(unit, 0))

    def arrived_sum(source, slots, unit, sems):
        for n, at in enumerate(sems):
            part = source.at[n, :, pl.ds(0, slots), :]
            pltpu.make_async_copy(part, part, second_recv.at[unit, at]).wait()

    def where_owner(unit, axis, run):
        if halved(unit, axis):
            pl.when(here.odd == 0)(run)
        else:
            run()

    def pass_on(unit):
        first, last = UNITS[unit][3]
        slots = width(unit) * (2 if halved(unit, last) else SIDE)

        def run():
            arrived_sum(near_ref.at[unit], slots, unit, range(4))
            for row in range(STRIP):
                total = near_ref[unit, 0, row, :slots, :]
                for o in range(1, SIDE):
                    total = total + near_ref[unit, o, row, :slots, :]
                middle_ref[unit, row, :slots, :] = total
            start_all(line(unit, 1))

        where_owner(unit, first, run)

    def end_second(unit):
        if UNITS[unit][3] == "plane":
            end_all(plane(unit))
        else:
            end_all(line(unit, 0))
            where_owner(unit, UNITS[unit][3][0], lambda: end_all(line(unit, 1)))

    def gather(unit):
        for o in range(8):
            if o == 0:
                first_copy(unit, 0, pl.ds(0, FULL)).wait()
            else:
                first_copy(unit, o, pl.ds(0, FULL)).wait_recv()
        ids = got_ref[unit * 8, SLAB:, :]
        for o in range(1, 8):
            ids = jnp.maximum(ids, got_ref[unit * 8 + o, SLAB:, :])
        ids = jnp.concatenate([ids[0:1, :], ids[1:2, :]], axis=1)
        hot = lax.broadcasted_iota(jnp.int32, (SLOTS, 256), 0).astype(jnp.float32) == ids
        hot = hot.astype(jnp.float32).astype(jnp.bfloat16)
        for row in range(STRIP):
            data = jnp.concatenate(
                [got_ref[unit * 8 + o, pl.ds(row, BLOCKS, stride=STRIP), :] for o in range(8)], axis=0
            )
            both = jnp.dot(hot, jnp.concatenate(split(data), axis=1), preferred_element_type=jnp.float32)
            dense_ref[unit, row] = both[:, :BLOCK] + both[:, BLOCK:]
        start_second(unit)

    def third_copies(unit):
        axis = UNITS[unit][2]
        if axis == "y":
            for o in range(4):
                down, c = o // 2, o % 2
                to = here.at(c=c)
                owner = here.c + 2 * down
                to["id"] = (owner, to["id"][1])
                yield o, to, to["c"] * 2 + down, (owner == here.y if c == 0 else False)
        else:
            for o in range(8):
                to = here.at(c=o % 2, **{axis: o // 2})
                yield o, to, to[axis] * 2 + to["c"], o == 0

    def third_refs(unit, o, to, at):
        axis = UNITS[unit][2]
        source = final_ref.at[unit, pl.ds(pl.multiple_of(at * 16, 16), 16), :]
        where = getattr(here, axis)
        target = got_final_ref.at[unit, where]
        away = remote(source, target, third_send.at[unit, o], third_recv.at[unit, where], to)
        return away, pltpu.make_async_copy(source, target, third_recv.at[unit, where])

    def reduce(unit):
        axis = UNITS[unit][2]
        slots = width(unit)

        def run():
            if UNITS[unit][3] == "plane":
                source, sems = sums_ref, range(16)
            else:
                source, sems = far_ref.at[unit], range(4, 8)
            arrived_sum(source, slots, unit, sems)
            for row in range(STRIP):
                total = source[0, row, :slots, :]
                for o in range(1, len(sems)):
                    total = total + source[o, row, :slots, :]
                final_ref[unit, pl.ds(row, slots, stride=STRIP), :] = total
            for o, to, at, own in third_copies(unit):
                away, home = third_refs(unit, o, to, at)
                if own is True:
                    home.start()
                elif own is False:
                    away.start()
                else:
                    pl.when(own)(home.start)
                    pl.when(jnp.logical_not(own))(away.start)

        if axis == "y":
            run()
        else:
            pl.when(here.odd == 0)(run)

    def end_third(unit):
        def run():
            for o, to, at, own in third_copies(unit):
                away, _ = third_refs(unit, o, to, at)
                if own is True:
                    continue
                if own is False:
                    away.wait_send()
                else:
                    pl.when(jnp.logical_not(own))(away.wait_send)

        if UNITS[unit][2] == "y":
            run()
        else:
            pl.when(here.odd == 0)(run)

    def finish(unit):
        array, half = UNITS[unit][:2]
        for step in range(SIDE):
            part = got_final_ref.at[unit, step]
            pltpu.make_async_copy(part, part, third_recv.at[unit, step]).wait()
            rows = slice(half * TILE + step * STRIP, half * TILE + (step + 1) * STRIP)
            out_ref[array, rows, :BLOCK] = got_final_ref[unit, step, :STRIP, :]
            out_ref[array, rows, BLOCK:] = got_final_ref[unit, step, STRIP:, :]

    def gather_inverses():
        gather(0)
        gather(1)

    compute(0, ((1, 0, SLAB // 2), (3, SLAB // 2, FULL)), ())
    quarters = [(g, g * SLAB // 4, (g + 1) * SLAB // 4) for g in range(3)] + [(3, SLAB * 3 // 4, FULL)]
    compute(1, quarters, ((0, gather_inverses), (2, lambda: gather(2))))
    pass_on(0)
    pass_on(1)
    gather(3)
    pass_on(2)
    for unit in range(3):
        reduce(unit)
    for unit in range(3):
        finish(unit)
    reduce(3)
    finish(3)
    for unit in range(4):
        for o in range(1, 8):
            first_copy(unit, o, pl.ds(0, FULL)).wait_send()
        end_second(unit)
        end_third(unit)


def fused(count, quadrants, *arrays):
    vmem = pl.BlockSpec(memory_space=pltpu.VMEM)
    smem = pl.BlockSpec(memory_space=pltpu.SMEM)
    dma = pltpu.SemaphoreType.DMA
    f32, bf16 = jnp.float32, jnp.bfloat16
    units = len(UNITS)
    return pl.pallas_call(
        fused_kernel,
        out_shape=jax.ShapeDtypeStruct((2, 64, 256), f32),
        in_specs=[smem, smem] + [pl.BlockSpec(memory_space=pl.ANY)] * 2 + [vmem] * (len(arrays) - 2),
        out_specs=vmem,
        scratch_shapes=[
            pltpu.VMEM((BLOCKS, BLOCK, BLOCK), f32),
            pltpu.VMEM((BLOCKS, BLOCK, BLOCK), f32),
            dma((2,)),
            pltpu.VMEM((NB * TILE, 256), bf16),
            pltpu.VMEM((NB, 256, 256), bf16),
            pltpu.VMEM((BLOCKS, 3, NB, BLOCK), f32),
            pltpu.VMEM((NB, GROUP * TILE, 256), bf16),
            pltpu.VMEM((units * 8, FULL, BLOCK), f32),
            pltpu.VMEM((units * 8, FULL, BLOCK), f32),
            pltpu.VMEM((units, STRIP, SLOTS, BLOCK), f32),
            pltpu.VMEM((units, SIDE, STRIP, 64, BLOCK), f32),
            pltpu.VMEM((units, STRIP, 64, BLOCK), f32),
            pltpu.VMEM((units, SIDE, STRIP, 16, BLOCK), f32),
            pltpu.VMEM((16, STRIP, 16, BLOCK), f32),
            pltpu.VMEM((units, 16 * STRIP, BLOCK), f32),
            pltpu.VMEM((units, SIDE, 2 * STRIP, BLOCK), f32),
            dma((units, 8)), dma((units, 8)),
            dma((units, 16)), dma((units, 16)),
            dma((units, 8)), dma((units, SIDE)),
        ],
        compiler_params=pltpu.CompilerParams(collective_id=0, has_side_effects=True, vmem_limit_bytes=56 << 20),
        name="coadd",
    )(count, quadrants, *arrays)


def on_device(
    image, variance, dest_patch, quadrant, coef_index, block_count, coef_table, row_taps, col_taps
):
    table = coef_table.transpose(2, 1, 0).reshape(-1, coef_table.shape[0])
    sums = fused(
        block_count[0], quadrant[0, 0], image[0, 0], variance[0, 0], row_taps, col_taps, table,
        coef_index[0], dest_patch[0], quadrant[0],
    )
    return sums[1][None], sums[0][None]


def solution(mesh):
    placed = (
        P("visit", "patch", None, None, None),
        P("visit", "patch", None, None, None),
        P("visit", "patch", None),
        P("visit", "patch", None),
        P("visit", "patch", None),
        P("visit", "patch"),
        P(),
        P(),
        P(),
    )
    return jax.shard_map(
        on_device,
        mesh=mesh,
        in_specs=placed,
        out_specs=(P("patch", "visit", None), P("patch", "visit", None)),
        check_vma=False,
    )
```

```python
import itertools

import jax
import jax.numpy as jnp
from jax import lax
from jax.experimental import pallas as pl
from jax.experimental.pallas import tpu as pltpu
from jax.sharding import PartitionSpec as P

BLOCK = 128
TAPS = 41
REACH = TAPS // 2
NB = 16
BLOCKS = 32
TILE = 32
WIN = 80
LEAD = 24
GROUP = 8
STRIP = 8
SIDE = 4
SLOTS = 128
SLAB = BLOCKS * STRIP
FULL = SLAB + STRIP
MESH = pl.DeviceIdType.MESH
UNITS = ((0, 0, "y", "xz"), (0, 1, "x", "zy"), (1, 0, "z", "xy"), (1, 1, "y", "plane"))
AXES = ("x", "y", "z")


def split(x):
    high = x.astype(jnp.bfloat16)
    return high, (x - high.astype(jnp.float32)).astype(jnp.bfloat16)


def build_bands(row_ref, col_ref, left_ref, right_ref):
    tap = lax.broadcasted_iota(jnp.int32, (TAPS, 256), 0)
    lane = lax.broadcasted_iota(jnp.int32, (TAPS, 256), 1)

    def place(parts, *found):
        hot = [f.astype(jnp.float32).astype(jnp.bfloat16) for f in found]
        return sum(jnp.dot(p, h, preferred_element_type=jnp.float32) for p, h in zip(parts, hot))

    at = LEAD + REACH - tap
    spread_rows = place(split(col_ref[...]), (lane == at) | (lane == at + 2 * WIN), lane == at + WIN)
    at = lax.rem(tap + (BLOCK - REACH), BLOCK)
    high, low = split(row_ref[...])
    row_high, row_low = place((high,), lane == at)[:, :BLOCK], place((low,), lane == at)[:, :BLOCK]
    near = lax.broadcasted_iota(jnp.int32, (BLOCK, BLOCK), 1) - lax.broadcasted_iota(jnp.int32, (BLOCK, BLOCK), 0)
    near = (near <= REACH) & (near >= -REACH)

    def roll(row, height):
        return pltpu.roll(jnp.broadcast_to(row, (height, row.shape[1])), 0, 1, stride=1, stride_axis=0)

    for k in range(NB):
        band = roll(spread_rows[k : k + 1, :], TILE)
        left_ref[k * TILE : (k + 1) * TILE, :] = band.astype(jnp.bfloat16)
        high = jnp.where(near, roll(row_high[k : k + 1, :], BLOCK), 0.0).astype(jnp.bfloat16)
        low = jnp.where(near, roll(row_low[k : k + 1, :], BLOCK), 0.0).astype(jnp.bfloat16)
        right_ref[k, :BLOCK, :BLOCK] = high
        right_ref[k, :BLOCK, BLOCK:] = low
        right_ref[k, BLOCK:, :BLOCK] = high
        right_ref[k, BLOCK:, BLOCK:] = jnp.zeros_like(low)


def build_polynomials(table_ref, index_ref, quadrant_ref, poly_ref):
    entry = lax.broadcasted_iota(jnp.int32, (table_ref.shape[1], BLOCK), 0)
    index = jnp.concatenate([index_ref[...]] * (BLOCK // BLOCKS), axis=1)
    hot = (entry == index).astype(jnp.float32).astype(jnp.bfloat16)
    rest, coefs = table_ref[...], None
    for _ in range(3):
        part = rest.astype(jnp.bfloat16)
        rest = rest - part.astype(jnp.float32)
        picked = jnp.dot(part, hot, preferred_element_type=jnp.float32)
        coefs = picked if coefs is None else coefs + picked
    column = lax.broadcasted_iota(jnp.int32, (NB, BLOCK), 1).astype(jnp.float32)
    own = (column + 0.5) / BLOCK - 1.0
    for b in range(BLOCKS):
        quadrant = quadrant_ref[b]
        down = (quadrant // 2).astype(jnp.float32)
        u = own + (quadrant % 2).astype(jnp.float32)
        a = [jnp.broadcast_to(coefs[m * NB : (m + 1) * NB, b : b + 1], (NB, BLOCK)) for m in range(6)]
        q = a[0] + u * (a[1] + u * a[3])
        s = a[2] + u * a[4]
        e = a[5]
        poly_ref[b, 0] = q + down * (s + down * e)
        poly_ref[b, 1] = s + (2.0 * down) * e
        poly_ref[b, 2] = e


def window(image_ref, block, tile):
    start = TILE * tile - LEAD
    low, high = max(start, 0), min(start + WIN, BLOCK)
    part = image_ref[block, low:high, :]
    pieces = []
    if low > start:
        pieces.append(jnp.zeros((low - start, BLOCK), jnp.float32))
    pieces.append(part)
    if high < start + WIN:
        pieces.append(jnp.zeros((start + WIN - high, BLOCK), jnp.float32))
    return jnp.concatenate(pieces, axis=0) if len(pieces) > 1 else part


def matched_tile(tile, first, image_ref, left_ref, right_ref, poly_ref, parts_ref, emit):
    for pair in range(GROUP // 2):
        both = jnp.concatenate(
            [window(image_ref, first + 2 * pair, tile), window(image_ref, first + 2 * pair + 1, tile)], axis=1
        )
        high, low = split(both)
        rhs = jnp.concatenate([high, high, low, jnp.zeros((256 - 3 * WIN, 2 * BLOCK), jnp.bfloat16)], axis=0)
        spread = jnp.dot(left_ref[...], rhs, preferred_element_type=jnp.float32)
        for side in range(2):
            high, low = split(spread[:, side * BLOCK : (side + 1) * BLOCK])
            at = (2 * pair + side) * TILE
            parts_ref[:, at : at + TILE, :BLOCK] = high.reshape(NB, TILE, BLOCK)
            parts_ref[:, at : at + TILE, BLOCK:] = low.reshape(NB, TILE, BLOCK)
    t = (lax.broadcasted_iota(jnp.int32, (TILE, BLOCK), 0).astype(jnp.float32) + (TILE * tile + 0.5)) / BLOCK - 1.0
    total = [None] * GROUP
    for k in range(NB):
        both = jnp.dot(parts_ref[k], right_ref[k], preferred_element_type=jnp.float32)
        basis = both[:, :BLOCK] + both[:, BLOCK:]
        for block in range(GROUP):
            q = poly_ref[first + block, 0, k : k + 1, :]
            s = poly_ref[first + block, 1, k : k + 1, :]
            e = poly_ref[first + block, 2, k : k + 1, :]
            term = (q + t * (s + t * e)) * basis[block * TILE : (block + 1) * TILE]
            total[block] = term if total[block] is None else total[block] + term
    for block in range(GROUP):
        emit(first + block, total[block])


class Here:
    def __init__(self):
        self.y = lax.axis_index("visit")
        place = lax.axis_index("patch")
        self.x, self.z, self.c = lax.div(place, 8), lax.rem(lax.div(place, 2), 4), lax.rem(place, 2)
        self.odd = lax.rem(self.y + self.c, 2)
        self.seen = {}

    def strip(self, axis):
        return getattr(self, axis) * 2 + self.c

    def at(self, c=0, **offsets):
        key = (c,) + tuple(offsets.get(axis, 0) for axis in AXES)
        known = all(isinstance(step, int) for step in key)
        if known and key in self.seen:
            return dict(self.seen[key])
        place = {
            axis: lax.rem(getattr(self, axis) + step, SIDE) if not isinstance(step, int) or step else getattr(self, axis)
            for axis, step in zip(AXES, key[1:])
        }
        place["c"] = lax.rem(self.c + c, 2) if c else self.c
        place["id"] = (place["y"], (place["x"] * SIDE + place["z"]) * 2 + place["c"])
        if known:
            self.seen[key] = place
        return dict(place)


def partners():
    found = set()
    for _, _, axis, later in UNITS:
        for step, c in itertools.product(range(SIDE), range(2)):
            found.add(tuple(step if a == axis else 0 for a in AXES) + (c,))
        others = [a for a in AXES if a != axis]
        for steps in itertools.product(range(SIDE), repeat=2):
            if later == "plane" or 0 in steps:
                to = dict(zip(others, steps))
                found.add(tuple(to.get(a, 0) for a in AXES) + (0,))
    found.discard((0, 0, 0, 0))
    return sorted(found)


def slot_rows(patches, quadrants, live, unit, here):
    _, _, axis, later = UNITS[unit]
    patch, quadrant = (jnp.concatenate([ref[...]] * 8, axis=1) for ref in (patches, quadrants))
    part = {"x": lax.div(patch, 8), "z": lax.rem(lax.div(patch, 2), 4)}
    sizes = {"x": 4, "z": 4, "y": 2}
    c = lax.rem(patch, 2)
    down, across = lax.div(quadrant, 2), lax.rem(quadrant, 2)
    part["y"] = down
    order = later if later != "plane" else "".join(a for a in "xzy" if a != axis)
    slot = part[order[0]] * sizes[order[1]] + part[order[1]]
    if axis == "y":
        slot = slot * 8 + c * 4 + down * 2 + across
    else:
        slot = slot * 16 + part[axis] * 4 + c * 2 + across
    lane = lax.broadcasted_iota(jnp.int32, slot.shape, 1)
    at = lane - here.strip(axis) * BLOCKS
    mine = (at >= 0) & (at < jnp.minimum(live, BLOCKS))
    slot = jnp.broadcast_to(jnp.where(mine, slot, -1).astype(jnp.float32), (STRIP, 256))
    row = lax.broadcasted_iota(jnp.int32, (STRIP, BLOCK), 0)
    return jnp.where(row == 0, slot[:, :BLOCK], slot[:, BLOCK:])


def fused_kernel(
    count_ref, quadrant_ref, image_hbm, variance_hbm, row_ref, col_ref, table_ref, index_ref, patches_ref, quadrants_ref,
    out_ref,
    image_ref, variance_ref, load_sem, left_ref, right_ref, poly_ref, parts_ref, strips_ref, got_ref, dense_ref, near_ref, middle_ref, far_ref, sums_ref,
    final_ref, got_final_ref,
    first_send, first_recv, second_send, second_recv, third_send, third_recv,
):
    def load_half(half):
        for core in range(2):
            rows = pl.ds(core * 64 + half * TILE, TILE)
            yield pltpu.make_async_copy(
                variance_hbm.at[:, rows, :], variance_ref.at[:, rows, :], load_sem.at[1 + half * 2 + core]
            )

    load_image = pltpu.make_async_copy(image_hbm, image_ref, load_sem.at[0])
    for half in range(2):
        for load in load_half(half):
            load.start()
    load_image.start()
    here = Here()
    barrier = pltpu.get_barrier_semaphore()
    all_partners = partners()
    here.at()
    for x, y, z, c in all_partners:
        pl.semaphore_signal(barrier, inc=1, device_id=here.at(x=x, y=y, z=z, c=c)["id"], device_id_type=MESH)

    live = count_ref[0]
    for unit in range(4):
        ids = slot_rows(patches_ref, quadrants_ref, live, unit, here)
        for at in range(8):
            strips_ref[unit * 8 + at, SLAB:, :] = ids

    def invert(half):
        def step(b, carry):
            flag = (b < live).astype(jnp.float32)
            rows = pl.ds(pl.multiple_of(b * STRIP, STRIP), STRIP)
            for core, step in itertools.product(range(2), range(SIDE)):
                first = core * 64 + half * TILE + step * STRIP
                strips_ref[half * 8 + step * 2 + core, rows, :] = flag / variance_ref[b, first : first + STRIP, :]
            return carry

        lax.fori_loop(0, BLOCKS, step, 0)

    def remote(src, dst, send, recv, to):
        return pltpu.make_async_remote_copy(
            src_ref=src, dst_ref=dst, send_sem=send, recv_sem=recv, device_id=to["id"], device_id_type=MESH
        )

    def first_copy(unit, o, rows):
        axis = UNITS[unit][2]
        to = here.at(c=o % 2, **{axis: o // 2})
        source = strips_ref.at[unit * 8 + to[axis] * 2 + to["c"], rows, :]
        target = got_ref.at[unit * 8 + here.strip(axis), rows, :]
        if o == 0:
            return pltpu.make_async_copy(source, target, first_recv.at[unit, 0])
        return remote(source, target, first_send.at[unit, o], first_recv.at[unit, o], to)

    for load in load_half(0):
        load.wait()
    invert(0)
    pl.semaphore_wait(barrier, len(all_partners))
    for o in range(8):
        first_copy(0, o, pl.ds(0, FULL)).start()
    for load in load_half(1):
        load.wait()
    invert(1)
    for o in range(8):
        first_copy(1, o, pl.ds(0, FULL)).start()
    build_bands(row_ref, col_ref, left_ref, right_ref)
    build_polynomials(table_ref, index_ref, quadrant_ref, poly_ref)
    load_image.wait()

    def compute(half, chunks, meanwhile):
        unit = 2 + half

        def step(group, carry):
            first = group * GROUP
            for core in range(2):

                def emit(b, total, core=core):
                    rows = pl.ds(pl.multiple_of(b * STRIP, STRIP), STRIP)
                    for step in range(SIDE):
                        at = step * 2 + core
                        strips_ref[unit * 8 + at, rows, :] = (
                            strips_ref[half * 8 + at, rows, :] * total[step * STRIP : (step + 1) * STRIP]
                        )

                matched_tile(core * 2 + half, first, image_ref, left_ref, right_ref, poly_ref, parts_ref, emit)

            for after, begin, end in chunks:

                @pl.when(group == after)
                def send(begin=begin, end=end):
                    for o in range(8):
                        first_copy(unit, o, pl.ds(begin, end - begin)).start()

            for after, run in meanwhile:
                pl.when(group == after)(run)
            return carry

        lax.fori_loop(0, BLOCKS // GROUP, step, 0)

    def choose(own, home, away):
        if own is True:
            home()
        elif own is False:
            away()
        else:
            pl.when(own)(home)
            pl.when(jnp.logical_not(own))(away)

    def nothing():
        pass

    def halved(unit, axis):
        return axis == "y" and UNITS[unit][2] != "y"

    def steps(unit, axis):
        if halved(unit, axis):
            for m in range(2):
                rise = here.odd + 2 * m
                to = here.at(y=rise)
                yield rise, to, lax.div(to["y"], 2), (here.odd == 0 if m == 0 else False)
        else:
            for o in range(SIDE):
                to = here.at(**{axis: o})
                yield o, to, to[axis], o == 0

    def width(unit):
        return 8 if UNITS[unit][2] == "y" else 16

    def line(unit, second):
        axis = UNITS[unit][3][second]
        slots = width(unit)
        if not second:
            slots = slots * (2 if halved(unit, UNITS[unit][3][1]) else SIDE)
        source, target = (middle_ref, far_ref) if second else (dense_ref, near_ref)
        for at, (o, to, share, own) in enumerate(steps(unit, axis)):
            part = source.at[unit, :, pl.ds(pl.multiple_of(share * slots, 8), slots), :]
            place = target.at[unit, o, :, pl.ds(0, slots), :]
            arrived = second_recv.at[unit, 4 * second + o]
            yield (
                pltpu.make_async_copy(part, place, arrived) if own is not False else None,
                remote(part, place, second_send.at[unit, 4 * second + at], arrived, to) if own is not True else None,
                own,
            )

    def plane(unit):
        slots = width(unit)
        first, last = (a for a in "xzy" if a != UNITS[unit][2])
        for at, ((o, to, share, own), (p, on, more, also)) in enumerate(
            itertools.product(steps(unit, first), steps(unit, last))
        ):
            to = dict(to, **{last: on[last]})
            to["id"] = (to["y"], (to["x"] * SIDE + to["z"]) * 2 + to["c"])
            base = pl.multiple_of((share * (2 if halved(unit, last) else SIDE) + more) * slots, 8)
            part = dense_ref.at[unit, :, pl.ds(base, slots), :]
            place = sums_ref.at[o * SIDE + p, :, pl.ds(0, slots), :]
            arrived = second_recv.at[unit, o * SIDE + p]
            own = False if own is False or also is False else also if own is True else own
            yield (
                pltpu.make_async_copy(part, place, arrived) if own is not False else None,
                remote(part, place, second_send.at[unit, at], arrived, to) if own is not True else None,
                own,
            )

    def start_all(copies):
        for home, away, own in copies:
            choose(own, home and home.start, away and away.start)

    def end_all(copies):
        for home, away, own in copies:
            choose(own, nothing, away and away.wait_send)

    def start_second(unit):
        start_all(plane(unit) if UNITS[unit][3] == "plane" else line(unit, 0))

    def arrived_sum(source, slots, unit, sems):
        for n, at in enumerate(sems):
            part = source.at[n, :, pl.ds(0, slots), :]
            pltpu.make_async_copy(part, part, second_recv.at[unit, at]).wait()

    def where_owner(unit, axis, run):
        if halved(unit, axis):
            pl.when(here.odd == 0)(run)
        else:
            run()

    def pass_on(unit):
        first, last = UNITS[unit][3]
        slots = width(unit) * (2 if halved(unit, last) else SIDE)

        def run():
            arrived_sum(near_ref.at[unit], slots, unit, range(4))
            for row in range(STRIP):
                total = near_ref[unit, 0, row, :slots, :]
                for o in range(1, SIDE):
                    total = total + near_ref[unit, o, row, :slots, :]
                middle_ref[unit, row, :slots, :] = total
            start_all(line(unit, 1))

        where_owner(unit, first, run)

    def end_second(unit):
        if UNITS[unit][3] == "plane":
            end_all(plane(unit))
        else:
            end_all(line(unit, 0))
            where_owner(unit, UNITS[unit][3][0], lambda: end_all(line(unit, 1)))

    def gather(unit):
        for o in range(8):
            if o == 0:
                first_copy(unit, 0, pl.ds(0, FULL)).wait()
            else:
                first_copy(unit, o, pl.ds(0, FULL)).wait_recv()
        ids = got_ref[unit * 8, SLAB:, :]
        for o in range(1, 8):
            ids = jnp.maximum(ids, got_ref[unit * 8 + o, SLAB:, :])
        ids = jnp.concatenate([ids[0:1, :], ids[1:2, :]], axis=1)
        hot = lax.broadcasted_iota(jnp.int32, (SLOTS, 256), 0).astype(jnp.float32) == ids
        hot = hot.astype(jnp.float32).astype(jnp.bfloat16)
        for row in range(STRIP):
            data = jnp.concatenate(
                [got_ref[unit * 8 + o, pl.ds(row, BLOCKS, stride=STRIP), :] for o in range(8)], axis=0
            )
            both = jnp.dot(hot, jnp.concatenate(split(data), axis=1), preferred_element_type=jnp.float32)
            dense_ref[unit, row] = both[:, :BLOCK] + both[:, BLOCK:]
        start_second(unit)

    def third_copies(unit):
        axis = UNITS[unit][2]
        if axis == "y":
            for o in range(4):
                down, c = o // 2, o % 2
                to = here.at(c=c)
                owner = here.c + 2 * down
                to["id"] = (owner, to["id"][1])
                yield o, to, to["c"] * 2 + down, (owner == here.y if c == 0 else False)
        else:
            for o in range(8):
                to = here.at(c=o % 2, **{axis: o // 2})
                yield o, to, to[axis] * 2 + to["c"], o == 0

    def third_refs(unit, o, to, at):
        axis = UNITS[unit][2]
        source = final_ref.at[unit, pl.ds(pl.multiple_of(at * 16, 16), 16), :]
        where = getattr(here, axis)
        target = got_final_ref.at[unit, where]
        away = remote(source, target, third_send.at[unit, o], third_recv.at[unit, where], to)
        return away, pltpu.make_async_copy(source, target, third_recv.at[unit, where])

    def reduce(unit):
        axis = UNITS[unit][2]
        slots = width(unit)

        def run():
            if UNITS[unit][3] == "plane":
                source, sems = sums_ref, range(16)
            else:
                source, sems = far_ref.at[unit], range(4, 8)
            arrived_sum(source, slots, unit, sems)
            for row in range(STRIP):
                total = source[0, row, :slots, :]
                for o in range(1, len(sems)):
                    total = total + source[o, row, :slots, :]
                final_ref[unit, pl.ds(row, slots, stride=STRIP), :] = total
            for o, to, at, own in third_copies(unit):
                away, home = third_refs(unit, o, to, at)
                if own is True:
                    home.start()
                elif own is False:
                    away.start()
                else:
                    pl.when(own)(home.start)
                    pl.when(jnp.logical_not(own))(away.start)

        if axis == "y":
            run()
        else:
            pl.when(here.odd == 0)(run)

    def end_third(unit):
        def run():
            for o, to, at, own in third_copies(unit):
                away, _ = third_refs(unit, o, to, at)
                if own is True:
                    continue
                if own is False:
                    away.wait_send()
                else:
                    pl.when(jnp.logical_not(own))(away.wait_send)

        if UNITS[unit][2] == "y":
            run()
        else:
            pl.when(here.odd == 0)(run)

    def finish(unit):
        array, half = UNITS[unit][:2]
        for step in range(SIDE):
            part = got_final_ref.at[unit, step]
            pltpu.make_async_copy(part, part, third_recv.at[unit, step]).wait()
            rows = slice(half * TILE + step * STRIP, half * TILE + (step + 1) * STRIP)
            out_ref[array, rows, :BLOCK] = got_final_ref[unit, step, :STRIP, :]
            out_ref[array, rows, BLOCK:] = got_final_ref[unit, step, STRIP:, :]

    def gather_inverses():
        gather(0)
        gather(1)

    compute(0, ((1, 0, SLAB // 2), (3, SLAB // 2, FULL)), ())
    quarters = [(g, g * SLAB // 4, (g + 1) * SLAB // 4) for g in range(3)] + [(3, SLAB * 3 // 4, FULL)]
    compute(1, quarters, ((0, gather_inverses), (2, lambda: gather(2))))
    pass_on(0)
    pass_on(1)
    gather(3)
    pass_on(2)
    for unit in range(4):
        reduce(unit)
    for unit in range(4):
        finish(unit)
    for unit in range(4):
        for o in range(1, 8):
            first_copy(unit, o, pl.ds(0, FULL)).wait_send()
        end_second(unit)
        end_third(unit)


def fused(count, quadrants, *arrays):
    vmem = pl.BlockSpec(memory_space=pltpu.VMEM)
    smem = pl.BlockSpec(memory_space=pltpu.SMEM)
    dma = pltpu.SemaphoreType.DMA
    f32, bf16 = jnp.float32, jnp.bfloat16
    units = len(UNITS)
    return pl.pallas_call(
        fused_kernel,
        out_shape=jax.ShapeDtypeStruct((2, 64, 256), f32),
        in_specs=[smem, smem] + [pl.BlockSpec(memory_space=pl.ANY)] * 2 + [vmem] * (len(arrays) - 2),
        out_specs=vmem,
        scratch_shapes=[
            pltpu.VMEM((BLOCKS, BLOCK, BLOCK), f32),
            pltpu.VMEM((BLOCKS, BLOCK, BLOCK), f32),
            dma((5,)),
            pltpu.VMEM((NB * TILE, 256), bf16),
            pltpu.VMEM((NB, 256, 256), bf16),
            pltpu.VMEM((BLOCKS, 3, NB, BLOCK), f32),
            pltpu.VMEM((NB, GROUP * TILE, 256), bf16),
            pltpu.VMEM((units * 8, FULL, BLOCK), f32),
            pltpu.VMEM((units * 8, FULL, BLOCK), f32),
            pltpu.VMEM((units, STRIP, SLOTS, BLOCK), f32),
            pltpu.VMEM((units, SIDE, STRIP, 64, BLOCK), f32),
            pltpu.VMEM((units, STRIP, 64, BLOCK), f32),
            pltpu.VMEM((units, SIDE, STRIP, 16, BLOCK), f32),
            pltpu.VMEM((16, STRIP, 16, BLOCK), f32),
            pltpu.VMEM((units, 16 * STRIP, BLOCK), f32),
            pltpu.VMEM((units, SIDE, 2 * STRIP, BLOCK), f32),
            dma((units, 8)), dma((units, 8)),
            dma((units, 16)), dma((units, 16)),
            dma((units, 8)), dma((units, SIDE)),
        ],
        compiler_params=pltpu.CompilerParams(collective_id=0, has_side_effects=True, vmem_limit_bytes=56 << 20),
        name="coadd",
    )(count, quadrants, *arrays)


def on_device(
    image, variance, dest_patch, quadrant, coef_index, block_count, coef_table, row_taps, col_taps
):
    table = coef_table.transpose(2, 1, 0).reshape(-1, coef_table.shape[0])
    sums = fused(
        block_count[0], quadrant[0, 0], image[0, 0], variance[0, 0], row_taps, col_taps, table,
        coef_index[0], dest_patch[0], quadrant[0],
    )
    return sums[1][None], sums[0][None]


def solution(mesh):
    placed = (
        P("visit", "patch", None, None, None),
        P("visit", "patch", None, None, None),
        P("visit", "patch", None),
        P("visit", "patch", None),
        P("visit", "patch", None),
        P("visit", "patch"),
        P(),
        P(),
        P(),
    )
    return jax.shard_map(
        on_device,
        mesh=mesh,
        in_specs=placed,
        out_specs=(P("patch", "visit", None), P("patch", "visit", None)),
        check_vma=False,
    )
```

```python
import itertools

import jax
import jax.numpy as jnp
from jax import lax
from jax.experimental import pallas as pl
from jax.experimental.pallas import tpu as pltpu
from jax.sharding import PartitionSpec as P

BLOCK = 128
TAPS = 41
REACH = TAPS // 2
NB = 16
BLOCKS = 32
TILE = 32
WIN = 80
LEAD = 24
GROUP = 8
STRIP = 8
SIDE = 4
SLOTS = 128
SLAB = BLOCKS * STRIP
FULL = SLAB + STRIP
MESH = pl.DeviceIdType.MESH
UNITS = ((0, 0, "y", "xz"), (0, 1, "x", "zy"), (1, 0, "z", "xy"), (1, 1, "y", "plane"))
AXES = ("x", "y", "z")


def split(x):
    high = x.astype(jnp.bfloat16)
    return high, (x - high.astype(jnp.float32)).astype(jnp.bfloat16)


def build_bands(row_ref, col_ref, left_ref, right_ref):
    tap = lax.broadcasted_iota(jnp.int32, (TAPS, 256), 0)
    lane = lax.broadcasted_iota(jnp.int32, (TAPS, 256), 1)

    def place(parts, *found):
        hot = [f.astype(jnp.float32).astype(jnp.bfloat16) for f in found]
        return sum(jnp.dot(p, h, preferred_element_type=jnp.float32) for p, h in zip(parts, hot))

    at = LEAD + REACH - tap
    spread_rows = place(split(col_ref[...]), (lane == at) | (lane == at + 2 * WIN), lane == at + WIN)
    at = lax.rem(tap + (BLOCK - REACH), BLOCK)
    high, low = split(row_ref[...])
    row_high, row_low = place((high,), lane == at)[:, :BLOCK], place((low,), lane == at)[:, :BLOCK]
    near = lax.broadcasted_iota(jnp.int32, (BLOCK, BLOCK), 1) - lax.broadcasted_iota(jnp.int32, (BLOCK, BLOCK), 0)
    near = (near <= REACH) & (near >= -REACH)

    def roll(row, height):
        return pltpu.roll(jnp.broadcast_to(row, (height, row.shape[1])), 0, 1, stride=1, stride_axis=0)

    for k in range(NB):
        band = roll(spread_rows[k : k + 1, :], TILE)
        left_ref[k * TILE : (k + 1) * TILE, :] = band.astype(jnp.bfloat16)
        high = jnp.where(near, roll(row_high[k : k + 1, :], BLOCK), 0.0).astype(jnp.bfloat16)
        low = jnp.where(near, roll(row_low[k : k + 1, :], BLOCK), 0.0).astype(jnp.bfloat16)
        right_ref[k, :BLOCK, :BLOCK] = high
        right_ref[k, :BLOCK, BLOCK:] = low
        right_ref[k, BLOCK:, :BLOCK] = high
        right_ref[k, BLOCK:, BLOCK:] = jnp.zeros_like(low)


def build_polynomials(table_ref, index_ref, quadrant_ref, poly_ref):
    entry = lax.broadcasted_iota(jnp.int32, (table_ref.shape[1], BLOCK), 0)
    index = jnp.concatenate([index_ref[...]] * (BLOCK // BLOCKS), axis=1)
    hot = (entry == index).astype(jnp.float32).astype(jnp.bfloat16)
    rest, coefs = table_ref[...], None
    for _ in range(3):
        part = rest.astype(jnp.bfloat16)
        rest = rest - part.astype(jnp.float32)
        picked = jnp.dot(part, hot, preferred_element_type=jnp.float32)
        coefs = picked if coefs is None else coefs + picked
    column = lax.broadcasted_iota(jnp.int32, (NB, BLOCK), 1).astype(jnp.float32)
    own = (column + 0.5) / BLOCK - 1.0
    for b in range(BLOCKS):
        quadrant = quadrant_ref[b]
        down = (quadrant // 2).astype(jnp.float32)
        u = own + (quadrant % 2).astype(jnp.float32)
        a = [jnp.broadcast_to(coefs[m * NB : (m + 1) * NB, b : b + 1], (NB, BLOCK)) for m in range(6)]
        q = a[0] + u * (a[1] + u * a[3])
        s = a[2] + u * a[4]
        e = a[5]
        poly_ref[b, 0] = q + down * (s + down * e)
        poly_ref[b, 1] = s + (2.0 * down) * e
        poly_ref[b, 2] = e


def window(image_ref, block, tile):
    start = TILE * tile - LEAD
    low, high = max(start, 0), min(start + WIN, BLOCK)
    part = image_ref[block, low:high, :]
    pieces = []
    if low > start:
        pieces.append(jnp.zeros((low - start, BLOCK), jnp.float32))
    pieces.append(part)
    if high < start + WIN:
        pieces.append(jnp.zeros((start + WIN - high, BLOCK), jnp.float32))
    return jnp.concatenate(pieces, axis=0) if len(pieces) > 1 else part


def matched_tile(tile, first, image_ref, left_ref, right_ref, poly_ref, parts_ref, emit):
    for pair in range(GROUP // 2):
        both = jnp.concatenate(
            [window(image_ref, first + 2 * pair, tile), window(image_ref, first + 2 * pair + 1, tile)], axis=1
        )
        high, low = split(both)
        rhs = jnp.concatenate([high, high, low, jnp.zeros((256 - 3 * WIN, 2 * BLOCK), jnp.bfloat16)], axis=0)
        spread = jnp.dot(left_ref[...], rhs, preferred_element_type=jnp.float32)
        for side in range(2):
            high, low = split(spread[:, side * BLOCK : (side + 1) * BLOCK])
            at = (2 * pair + side) * TILE
            parts_ref[:, at : at + TILE, :BLOCK] = high.reshape(NB, TILE, BLOCK)
            parts_ref[:, at : at + TILE, BLOCK:] = low.reshape(NB, TILE, BLOCK)
    t = (lax.broadcasted_iota(jnp.int32, (TILE, BLOCK), 0).astype(jnp.float32) + (TILE * tile + 0.5)) / BLOCK - 1.0
    total = [None] * GROUP
    for k in range(NB):
        both = jnp.dot(parts_ref[k], right_ref[k], preferred_element_type=jnp.float32)
        basis = both[:, :BLOCK] + both[:, BLOCK:]
        for block in range(GROUP):
            q = poly_ref[first + block, 0, k : k + 1, :]
            s = poly_ref[first + block, 1, k : k + 1, :]
            e = poly_ref[first + block, 2, k : k + 1, :]
            term = (q + t * (s + t * e)) * basis[block * TILE : (block + 1) * TILE]
            total[block] = term if total[block] is None else total[block] + term
    for block in range(GROUP):
        emit(first + block, total[block])


class Here:
    def __init__(self):
        self.y = lax.axis_index("visit")
        place = lax.axis_index("patch")
        self.x, self.z, self.c = lax.div(place, 8), lax.rem(lax.div(place, 2), 4), lax.rem(place, 2)
        self.odd = lax.rem(self.y + self.c, 2)
        self.seen = {}

    def strip(self, axis):
        return getattr(self, axis) * 2 + self.c

    def at(self, c=0, **offsets):
        key = (c,) + tuple(offsets.get(axis, 0) for axis in AXES)
        known = all(isinstance(step, int) for step in key)
        if known and key in self.seen:
            return dict(self.seen[key])
        place = {
            axis: lax.rem(getattr(self, axis) + step, SIDE) if not isinstance(step, int) or step else getattr(self, axis)
            for axis, step in zip(AXES, key[1:])
        }
        place["c"] = lax.rem(self.c + c, 2) if c else self.c
        place["id"] = (place["y"], (place["x"] * SIDE + place["z"]) * 2 + place["c"])
        if known:
            self.seen[key] = place
        return dict(place)


def partners():
    found = set()
    for _, _, axis, later in UNITS:
        for step, c in itertools.product(range(SIDE), range(2)):
            found.add(tuple(step if a == axis else 0 for a in AXES) + (c,))
        others = [a for a in AXES if a != axis]
        for steps in itertools.product(range(SIDE), repeat=2):
            if later == "plane" or 0 in steps:
                to = dict(zip(others, steps))
                found.add(tuple(to.get(a, 0) for a in AXES) + (0,))
    found.discard((0, 0, 0, 0))
    return sorted(found)


def slot_rows(patches, quadrants, live, unit, here):
    _, _, axis, later = UNITS[unit]
    patch, quadrant = (jnp.concatenate([ref[...]] * 8, axis=1) for ref in (patches, quadrants))
    part = {"x": lax.div(patch, 8), "z": lax.rem(lax.div(patch, 2), 4)}
    sizes = {"x": 4, "z": 4, "y": 2}
    c = lax.rem(patch, 2)
    down, across = lax.div(quadrant, 2), lax.rem(quadrant, 2)
    part["y"] = down
    order = later if later != "plane" else "".join(a for a in "xzy" if a != axis)
    slot = part[order[0]] * sizes[order[1]] + part[order[1]]
    if axis == "y":
        slot = slot * 8 + c * 4 + down * 2 + across
    else:
        slot = slot * 16 + part[axis] * 4 + c * 2 + across
    lane = lax.broadcasted_iota(jnp.int32, slot.shape, 1)
    at = lane - here.strip(axis) * BLOCKS
    mine = (at >= 0) & (at < jnp.minimum(live, BLOCKS))
    slot = jnp.broadcast_to(jnp.where(mine, slot, -1).astype(jnp.float32), (STRIP, 256))
    row = lax.broadcasted_iota(jnp.int32, (STRIP, BLOCK), 0)
    return jnp.where(row == 0, slot[:, :BLOCK], slot[:, BLOCK:])


def fused_kernel(
    count_ref, quadrant_ref, image_hbm, variance_hbm, row_ref, col_ref, table_ref, index_ref, patches_ref, quadrants_ref,
    out_ref,
    image_ref, variance_ref, load_sem, left_ref, right_ref, poly_ref, parts_ref, strips_ref, got_ref, dense_ref, near_ref, middle_ref, far_ref, sums_ref,
    final_ref, got_final_ref,
    first_send, first_recv, second_send, second_recv, third_send, third_recv,
):
    def load_half(half):
        for core in range(2):
            rows = pl.ds(core * 64 + half * TILE, TILE)
            yield pltpu.make_async_copy(
                variance_hbm.at[:, rows, :], variance_ref.at[:, rows, :], load_sem.at[1 + half * 2 + core]
            )

    load_image = pltpu.make_async_copy(image_hbm, image_ref, load_sem.at[0])
    for half in range(2):
        for load in load_half(half):
            load.start()
    load_image.start()
    here = Here()
    barrier = pltpu.get_barrier_semaphore()
    all_partners = partners()
    here.at()
    for x, y, z, c in all_partners:
        pl.semaphore_signal(barrier, inc=1, device_id=here.at(x=x, y=y, z=z, c=c)["id"], device_id_type=MESH)

    live = count_ref[0]
    for unit in range(4):
        ids = slot_rows(patches_ref, quadrants_ref, live, unit, here)
        for at in range(8):
            strips_ref[unit * 8 + at, SLAB:, :] = ids

    def invert(half):
        def step(b, carry):
            flag = (b < live).astype(jnp.float32)
            rows = pl.ds(pl.multiple_of(b * STRIP, STRIP), STRIP)
            for core, step in itertools.product(range(2), range(SIDE)):
                first = core * 64 + half * TILE + step * STRIP
                strips_ref[half * 8 + step * 2 + core, rows, :] = flag / variance_ref[b, first : first + STRIP, :]
            return carry

        lax.fori_loop(0, BLOCKS, step, 0)

    def remote(src, dst, send, recv, to):
        return pltpu.make_async_remote_copy(
            src_ref=src, dst_ref=dst, send_sem=send, recv_sem=recv, device_id=to["id"], device_id_type=MESH
        )

    def first_copy(unit, o, rows):
        axis = UNITS[unit][2]
        to = here.at(c=o % 2, **{axis: o // 2})
        source = strips_ref.at[unit * 8 + to[axis] * 2 + to["c"], rows, :]
        target = got_ref.at[unit * 8 + here.strip(axis), rows, :]
        if o == 0:
            return pltpu.make_async_copy(source, target, first_recv.at[unit, 0])
        return remote(source, target, first_send.at[unit, o], first_recv.at[unit, o], to)

    build_bands(row_ref, col_ref, left_ref, right_ref)
    for load in load_half(0):
        load.wait()
    invert(0)
    pl.semaphore_wait(barrier, len(all_partners))
    for o in range(8):
        first_copy(0, o, pl.ds(0, FULL)).start()
    for load in load_half(1):
        load.wait()
    invert(1)
    for o in range(8):
        first_copy(1, o, pl.ds(0, FULL)).start()
    build_polynomials(table_ref, index_ref, quadrant_ref, poly_ref)
    load_image.wait()

    def compute(half, chunks, meanwhile):
        unit = 2 + half

        def step(group, carry):
            first = group * GROUP
            for core in range(2):

                def emit(b, total, core=core):
                    rows = pl.ds(pl.multiple_of(b * STRIP, STRIP), STRIP)
                    for step in range(SIDE):
                        at = step * 2 + core
                        strips_ref[unit * 8 + at, rows, :] = (
                            strips_ref[half * 8 + at, rows, :] * total[step * STRIP : (step + 1) * STRIP]
                        )

                matched_tile(core * 2 + half, first, image_ref, left_ref, right_ref, poly_ref, parts_ref, emit)

            for after, begin, end in chunks:

                @pl.when(group == after)
                def send(begin=begin, end=end):
                    for o in range(8):
                        first_copy(unit, o, pl.ds(begin, end - begin)).start()

            for after, run in meanwhile:
                pl.when(group == after)(run)
            return carry

        lax.fori_loop(0, BLOCKS // GROUP, step, 0)

    def choose(own, home, away):
        if own is True:
            home()
        elif own is False:
            away()
        else:
            pl.when(own)(home)
            pl.when(jnp.logical_not(own))(away)

    def nothing():
        pass

    def halved(unit, axis):
        return axis == "y" and UNITS[unit][2] != "y"

    def steps(unit, axis):
        if halved(unit, axis):
            for m in range(2):
                rise = here.odd + 2 * m
                to = here.at(y=rise)
                yield rise, to, lax.div(to["y"], 2), (here.odd == 0 if m == 0 else False)
        else:
            for o in range(SIDE):
                to = here.at(**{axis: o})
                yield o, to, to[axis], o == 0

    def width(unit):
        return 8 if UNITS[unit][2] == "y" else 16

    def line(unit, second):
        axis = UNITS[unit][3][second]
        slots = width(unit)
        if not second:
            slots = slots * (2 if halved(unit, UNITS[unit][3][1]) else SIDE)
        source, target = (middle_ref, far_ref) if second else (dense_ref, near_ref)
        for at, (o, to, share, own) in enumerate(steps(unit, axis)):
            part = source.at[unit, :, pl.ds(pl.multiple_of(share * slots, 8), slots), :]
            place = target.at[unit, o, :, pl.ds(0, slots), :]
            arrived = second_recv.at[unit, 4 * second + o]
            yield (
                pltpu.make_async_copy(part, place, arrived) if own is not False else None,
                remote(part, place, second_send.at[unit, 4 * second + at], arrived, to) if own is not True else None,
                own,
            )

    def plane(unit):
        slots = width(unit)
        first, last = (a for a in "xzy" if a != UNITS[unit][2])
        for at, ((o, to, share, own), (p, on, more, also)) in enumerate(
            itertools.product(steps(unit, first), steps(unit, last))
        ):
            to = dict(to, **{last: on[last]})
            to["id"] = (to["y"], (to["x"] * SIDE + to["z"]) * 2 + to["c"])
            base = pl.multiple_of((share * (2 if halved(unit, last) else SIDE) + more) * slots, 8)
            part = dense_ref.at[unit, :, pl.ds(base, slots), :]
            place = sums_ref.at[o * SIDE + p, :, pl.ds(0, slots), :]
            arrived = second_recv.at[unit, o * SIDE + p]
            own = False if own is False or also is False else also if own is True else own
            yield (
                pltpu.make_async_copy(part, place, arrived) if own is not False else None,
                remote(part, place, second_send.at[unit, at], arrived, to) if own is not True else None,
                own,
            )

    def start_all(copies):
        for home, away, own in copies:
            choose(own, home and home.start, away and away.start)

    def end_all(copies):
        for home, away, own in copies:
            choose(own, nothing, away and away.wait_send)

    def start_second(unit):
        start_all(plane(unit) if UNITS[unit][3] == "plane" else line(unit, 0))

    def arrived_sum(source, slots, unit, sems):
        for n, at in enumerate(sems):
            part = source.at[n, :, pl.ds(0, slots), :]
            pltpu.make_async_copy(part, part, second_recv.at[unit, at]).wait()

    def where_owner(unit, axis, run):
        if halved(unit, axis):
            pl.when(here.odd == 0)(run)
        else:
            run()

    def pass_on(unit):
        first, last = UNITS[unit][3]
        slots = width(unit) * (2 if halved(unit, last) else SIDE)

        def run():
            arrived_sum(near_ref.at[unit], slots, unit, range(4))
            for row in range(STRIP):
                total = near_ref[unit, 0, row, :slots, :]
                for o in range(1, SIDE):
                    total = total + near_ref[unit, o, row, :slots, :]
                middle_ref[unit, row, :slots, :] = total
            start_all(line(unit, 1))

        where_owner(unit, first, run)

    def end_second(unit):
        if UNITS[unit][3] == "plane":
            end_all(plane(unit))
        else:
            end_all(line(unit, 0))
            where_owner(unit, UNITS[unit][3][0], lambda: end_all(line(unit, 1)))

    def gather(unit):
        for o in range(8):
            if o == 0:
                first_copy(unit, 0, pl.ds(0, FULL)).wait()
            else:
                first_copy(unit, o, pl.ds(0, FULL)).wait_recv()
        ids = got_ref[unit * 8, SLAB:, :]
        for o in range(1, 8):
            ids = jnp.maximum(ids, got_ref[unit * 8 + o, SLAB:, :])
        ids = jnp.concatenate([ids[0:1, :], ids[1:2, :]], axis=1)
        hot = lax.broadcasted_iota(jnp.int32, (SLOTS, 256), 0).astype(jnp.float32) == ids
        hot = hot.astype(jnp.float32).astype(jnp.bfloat16)
        for row in range(STRIP):
            data = jnp.concatenate(
                [got_ref[unit * 8 + o, pl.ds(row, BLOCKS, stride=STRIP), :] for o in range(8)], axis=0
            )
            both = jnp.dot(hot, jnp.concatenate(split(data), axis=1), preferred_element_type=jnp.float32)
            dense_ref[unit, row] = both[:, :BLOCK] + both[:, BLOCK:]
        start_second(unit)

    def third_copies(unit):
        axis = UNITS[unit][2]
        if axis == "y":
            for o in range(4):
                down, c = o // 2, o % 2
                to = here.at(c=c)
                owner = here.c + 2 * down
                to["id"] = (owner, to["id"][1])
                yield o, to, to["c"] * 2 + down, (owner == here.y if c == 0 else False)
        else:
            for o in range(8):
                to = here.at(c=o % 2, **{axis: o // 2})
                yield o, to, to[axis] * 2 + to["c"], o == 0

    def third_refs(unit, o, to, at):
        axis = UNITS[unit][2]
        source = final_ref.at[unit, pl.ds(pl.multiple_of(at * 16, 16), 16), :]
        where = getattr(here, axis)
        target = got_final_ref.at[unit, where]
        away = remote(source, target, third_send.at[unit, o], third_recv.at[unit, where], to)
        return away, pltpu.make_async_copy(source, target, third_recv.at[unit, where])

    def reduce(unit):
        axis = UNITS[unit][2]
        slots = width(unit)

        def run():
            if UNITS[unit][3] == "plane":
                source, sems = sums_ref, range(16)
            else:
                source, sems = far_ref.at[unit], range(4, 8)
            arrived_sum(source, slots, unit, sems)
            for row in range(STRIP):
                total = source[0, row, :slots, :]
                for o in range(1, len(sems)):
                    total = total + source[o, row, :slots, :]
                final_ref[unit, pl.ds(row, slots, stride=STRIP), :] = total
            for o, to, at, own in third_copies(unit):
                away, home = third_refs(unit, o, to, at)
                if own is True:
                    home.start()
                elif own is False:
                    away.start()
                else:
                    pl.when(own)(home.start)
                    pl.when(jnp.logical_not(own))(away.start)

        if axis == "y":
            run()
        else:
            pl.when(here.odd == 0)(run)

    def end_third(unit):
        def run():
            for o, to, at, own in third_copies(unit):
                away, _ = third_refs(unit, o, to, at)
                if own is True:
                    continue
                if own is False:
                    away.wait_send()
                else:
                    pl.when(jnp.logical_not(own))(away.wait_send)

        if UNITS[unit][2] == "y":
            run()
        else:
            pl.when(here.odd == 0)(run)

    def finish(unit):
        array, half = UNITS[unit][:2]
        for step in range(SIDE):
            part = got_final_ref.at[unit, step]
            pltpu.make_async_copy(part, part, third_recv.at[unit, step]).wait()
            rows = slice(half * TILE + step * STRIP, half * TILE + (step + 1) * STRIP)
            out_ref[array, rows, :BLOCK] = got_final_ref[unit, step, :STRIP, :]
            out_ref[array, rows, BLOCK:] = got_final_ref[unit, step, STRIP:, :]

    def gather_inverses():
        gather(0)
        gather(1)

    compute(0, ((1, 0, SLAB // 2), (3, SLAB // 2, FULL)), ())
    quarters = [(g, g * SLAB // 4, (g + 1) * SLAB // 4) for g in range(3)] + [(3, SLAB * 3 // 4, FULL)]
    compute(1, quarters, ((0, gather_inverses), (2, lambda: gather(2))))
    pass_on(0)
    pass_on(1)
    gather(3)
    pass_on(2)
    for unit in range(4):
        reduce(unit)
    for unit in range(4):
        finish(unit)
    for unit in range(4):
        for o in range(1, 8):
            first_copy(unit, o, pl.ds(0, FULL)).wait_send()
        end_second(unit)
        end_third(unit)


def fused(count, quadrants, *arrays):
    vmem = pl.BlockSpec(memory_space=pltpu.VMEM)
    smem = pl.BlockSpec(memory_space=pltpu.SMEM)
    dma = pltpu.SemaphoreType.DMA
    f32, bf16 = jnp.float32, jnp.bfloat16
    units = len(UNITS)
    return pl.pallas_call(
        fused_kernel,
        out_shape=jax.ShapeDtypeStruct((2, 64, 256), f32),
        in_specs=[smem, smem] + [pl.BlockSpec(memory_space=pl.ANY)] * 2 + [vmem] * (len(arrays) - 2),
        out_specs=vmem,
        scratch_shapes=[
            pltpu.VMEM((BLOCKS, BLOCK, BLOCK), f32),
            pltpu.VMEM((BLOCKS, BLOCK, BLOCK), f32),
            dma((5,)),
            pltpu.VMEM((NB * TILE, 256), bf16),
            pltpu.VMEM((NB, 256, 256), bf16),
            pltpu.VMEM((BLOCKS, 3, NB, BLOCK), f32),
            pltpu.VMEM((NB, GROUP * TILE, 256), bf16),
            pltpu.VMEM((units * 8, FULL, BLOCK), f32),
            pltpu.VMEM((units * 8, FULL, BLOCK), f32),
            pltpu.VMEM((units, STRIP, SLOTS, BLOCK), f32),
            pltpu.VMEM((units, SIDE, STRIP, 64, BLOCK), f32),
            pltpu.VMEM((units, STRIP, 64, BLOCK), f32),
            pltpu.VMEM((units, SIDE, STRIP, 16, BLOCK), f32),
            pltpu.VMEM((16, STRIP, 16, BLOCK), f32),
            pltpu.VMEM((units, 16 * STRIP, BLOCK), f32),
            pltpu.VMEM((units, SIDE, 2 * STRIP, BLOCK), f32),
            dma((units, 8)), dma((units, 8)),
            dma((units, 16)), dma((units, 16)),
            dma((units, 8)), dma((units, SIDE)),
        ],
        compiler_params=pltpu.CompilerParams(collective_id=0, has_side_effects=True, vmem_limit_bytes=56 << 20),
        name="coadd",
    )(count, quadrants, *arrays)


def on_device(
    image, variance, dest_patch, quadrant, coef_index, block_count, coef_table, row_taps, col_taps
):
    table = coef_table.transpose(2, 1, 0).reshape(-1, coef_table.shape[0])
    sums = fused(
        block_count[0], quadrant[0, 0], image[0, 0], variance[0, 0], row_taps, col_taps, table,
        coef_index[0], dest_patch[0], quadrant[0],
    )
    return sums[1][None], sums[0][None]


def solution(mesh):
    placed = (
        P("visit", "patch", None, None, None),
        P("visit", "patch", None, None, None),
        P("visit", "patch", None),
        P("visit", "patch", None),
        P("visit", "patch", None),
        P("visit", "patch"),
        P(),
        P(),
        P(),
    )
    return jax.shard_map(
        on_device,
        mesh=mesh,
        in_specs=placed,
        out_specs=(P("patch", "visit", None), P("patch", "visit", None)),
        check_vma=False,
    )
```
